768 devices in a mesh: group: 8 (over y), blk: 32 (over x, z_lo, core), att: 3 (over z_hi).
Axes of the slice: x: 4, y: 8, z: 12 (z_hi: 3, z_lo: 4; z = z_hi * 4 + z_lo), core: 2. Of those that a mesh axis runs over, the one named last changes fastest.
Arguments:
- tokens: bfloat16 [32768, 4096], P(('group', 'blk')), may hold values from -6 to 6
- routed_experts: int32 [32768, 8], P(('group', 'blk')), may hold values from 0 to 127, all different within a row; in each aligned block of 128 rows (0 to 127, 128 to 255, ...) at most 16 rows name the same one
- act_cotangent: bfloat16 [32768, 8, 768], P(('group', 'blk'), None, 'att'), may hold values from -0.625 to 0.625
- weight_codes: bfloat16 [4096, 8, 2, 768], P('blk', 'group', None, 'att'), may hold values from -0.09375 to 0.09375
- weight_scales: bfloat16 [32, 8, 2, 6], P('blk', 'group', None, 'att'), may hold values from 0.3984375 to 2.5
Outputs:
- gate_up_gradient: bfloat16 [4096, 8, 2, 768], P('blk', 'group', None, 'att')
The draws below stay inside these ranges and needn't reach their ends.
Inputs may be any that keep to these rules, and one draw needn't show every extreme that they name: `routed_experts`: each row names 8 different experts. Among the 128 rows of one device (aligned blocks of 128 rows), no expert is named by more than 16 rows, a bound that some block reaches.
All inputs are finite; a program needn't handle non-finite values.
Results may differ from the reference program's by a relative error of at most 0.023.
Values may be sent and summed in bfloat16 or wider, within the bound.
A program may use at most 64 MiB of HBM per device.

```python
import math
import jax
import jax.numpy as jnp
import numpy as np
from jax import lax

D = 4096
EXPERTS = 128
TOPK = 8
H = 768
QB = 128
TOK_DEV = 128
CAP = 16
FLIGHT = 8
CYCLE_LEN = 32
TOKENS = 32768


def level_of(key, extent, shards, low, top_value):
    def one(dim, parts):
        draws = jax.random.uniform(jax.random.fold_in(jax.random.fold_in(key, 6), dim), (parts,), jnp.float32, low / len(shards), top_value / len(shards))
        return jnp.repeat(jnp.exp(draws), extent[dim] // parts).reshape((-1,) + (1,) * (len(extent) - dim - 1))

    gain = one(*shards[0])
    for cut in shards[1:]:
        gain = gain * one(*cut)
    return gain


def routed_block(rng, own, number, rows, count, top, limit, skew):
    sequence = jax.random.permutation(rng, count)
    packed, common = load_shares(count, rows * top, limit, skew, True), load_shares(count, rows * top, limit, skew, False)
    places = jnp.arange(count)

    def named(sizes, offset_by):
        used = int((sizes > 0).sum())
        fixed = max(1, used // 4)
        passed = fixed + (places - fixed + offset_by * (used - fixed)) % max(1, count - fixed)
        return jnp.zeros((count,), jnp.int32).at[sequence[jnp.where(places < fixed, places, passed)]].set(jnp.asarray(sizes, jnp.int32))

    sizes = jnp.where(number % 4 == 0, named(packed, number // 4), named(common, number - number // 4 - 1))
    mixed = jax.random.permutation(jax.random.fold_in(own, 3), count)
    source_of, sink = mixed[0:count // 2 * 2:2], mixed[1:count // 2 * 2:2]
    margin = jnp.minimum(sizes[source_of] - 1, limit - sizes[sink]) // 2
    margin = jnp.where((source_of == sequence[0]) | (sink == sequence[0]) | (sizes[sink] == 0), 0, jnp.maximum(margin, 0))
    passed = jax.random.randint(jax.random.fold_in(own, 4), (count // 2,), 0, 1 << 20) % (margin + 1)
    sizes = sizes.at[source_of].add(-passed).at[sink].add(passed)
    members = jnp.searchsorted(jnp.cumsum(sizes), jnp.arange(rows * top), side="right").astype(jnp.int32)
    grid = members.reshape(top, rows).T
    grid = grid[jax.random.permutation(jax.random.fold_in(own, 1), rows)]
    offset_by = jax.random.randint(jax.random.fold_in(own, 2), (rows, 1), 0, top)
    return jnp.take_along_axis(grid, (jnp.arange(top)[None, :] + offset_by) % top, axis=1)


def load_shares(count, total, bound, skew, full):
    loads = [(1 << 20) // math.isqrt(rank ** skew) + 1 for rank in range(1, count + 1)]
    largest = bound if full else min(bound, max(-(-total // count), total * loads[0] // sum(loads)))
    least = 1 if total - largest >= count - 1 else 0
    holding, surplus = [largest] + [least] * (count - 1), total - largest - least * (count - 1)
    while surplus > 0:
        candidates = [i for i in range(1, count) if holding[i] < largest] or [i for i in range(1, count) if holding[i] < bound]
        whole, remaining = sum([loads[i] for i in candidates]), surplus
        for i in candidates:
            extra = min(bound - holding[i], max(1, remaining * loads[i] // whole), surplus)
            holding[i] = holding[i] + extra
            surplus = surplus - extra
    return np.array(holding)


def scatter_about(rng, extent, scale, limit, shards=(), kind=jnp.bfloat16):
    gain = level_of(rng, extent, shards, -0.22, 0.18) if shards else 1.0
    values = jax.random.normal(rng, extent, jnp.float32) * scale * gain
    return jnp.minimum(jnp.maximum(values, -limit), limit).astype(kind)


def setup_inputs(seed: int = 0) -> dict:
    key_of = jax.random.split(jax.random.key(seed), 6)
    tokens = scatter_about(key_of[0], (TOKENS, D), 1.0, 6.0, ((0, 256),))
    routed_experts_keys = jax.random.split(jax.random.fold_in(key_of[1], 1), TOKENS // TOK_DEV)
    routed_experts_turns = jax.random.permutation(jax.random.fold_in(key_of[1], 3), TOKENS // TOK_DEV)
    routed_experts = jax.vmap(lambda own, number: routed_block(jax.random.fold_in(key_of[1], 2), own, number, TOK_DEV, EXPERTS, TOPK, CAP, 2))(routed_experts_keys, routed_experts_turns).reshape((TOKENS, TOPK))
    act_cotangent = scatter_about(key_of[2], (TOKENS, TOPK, H), (2.0 * (EXPERTS / (TOKENS * TOPK)) ** 0.5), 0.625, ((0, 256), (2, 3)))
    weight_codes = scatter_about(key_of[3], (D, FLIGHT, 2, H), D ** -0.5, 0.09375, ((0, 32), (1, 8), (3, 3)))
    weight_scales = jnp.clip(jnp.exp(math.log(2.5) - 1.8364954 * jax.random.uniform(key_of[4], (D // QB, FLIGHT, 2, H // QB), jnp.float32) ** level_of(key_of[4], (D // QB, FLIGHT, 2, H // QB), ((0, 32), (1, 8), (3, 3)), -0.2, 0.2)), 0.3984375, 2.5).astype(jnp.bfloat16)
    return dict(tokens=tokens, routed_experts=routed_experts, act_cotangent=act_cotangent, weight_codes=weight_codes, weight_scales=weight_scales)


def reference(tokens, routed_experts, act_cotangent, weight_codes, weight_scales):
    sources = TOKENS // TOK_DEV
    token_blocks = tokens.astype(jnp.float32).reshape(sources, TOK_DEV, D)
    id_blocks = routed_experts.reshape(sources, TOK_DEV, TOPK)
    cotangent_blocks = act_cotangent.astype(jnp.float32).reshape(sources, TOK_DEV, TOPK, H)
    slot_index = jnp.arange(CAP, dtype=jnp.int32).astype(jnp.float32)

    def one_expert(expert):
        matches = (id_blocks == expert).astype(jnp.float32)
        chosen = jnp.sum(matches, axis=2)
        position = jnp.cumsum(chosen, axis=1) - 1.0
        selector = chosen[:, None, :] * (position[:, None, :] == slot_index[None, :, None]).astype(jnp.float32)
        sent_tokens = jnp.einsum("sct,std->scd", selector, token_blocks)
        pair_cotangent = jnp.einsum("stk,stkh->sth", matches, cotangent_blocks)
        sent_cotangent = jnp.einsum("sct,sth->sch", selector, pair_cotangent)
        code_values = lax.dynamic_index_in_dim(weight_codes, expert, 1, keepdims=False).astype(jnp.float32)
        scale_values = lax.dynamic_index_in_dim(weight_scales, expert, 1, keepdims=False).astype(jnp.float32)
        expanded = jnp.repeat(jnp.repeat(scale_values, QB, axis=0), QB, axis=2)
        weights = lax.optimization_barrier((code_values * expanded).astype(jnp.bfloat16)).astype(jnp.float32)
        gate_up = jnp.einsum("scd,djh->scjh", sent_tokens, weights)
        gate_pre = gate_up[:, :, 0]
        up_pre = gate_up[:, :, 1]
        sigmoid_gate = jax.nn.sigmoid(gate_pre)
        gate_cotangent = sent_cotangent * up_pre * sigmoid_gate * (1.0 + gate_pre * (1.0 - sigmoid_gate))
        up_cotangent = sent_cotangent * gate_pre * sigmoid_gate
        pre_cotangent = jnp.stack([gate_cotangent, up_cotangent], axis=2)
        pre_cotangent = lax.optimization_barrier(pre_cotangent.astype(jnp.bfloat16)).astype(jnp.float32)
        cycle_tokens = sent_tokens.reshape(sources // CYCLE_LEN, CYCLE_LEN, CAP, D)
        cycle_cotangent = pre_cotangent.reshape(sources // CYCLE_LEN, CYCLE_LEN, CAP, 2, H)

        def add_position(running, cycle_place):
            here_tokens = lax.dynamic_index_in_dim(cycle_tokens, cycle_place, 1, keepdims=False)
            here_cotangent = lax.dynamic_index_in_dim(cycle_cotangent, cycle_place, 1, keepdims=False)
            position_term = jnp.einsum("gcd,gcjh->djh", here_tokens, here_cotangent)
            position_term = lax.optimization_barrier(position_term.astype(jnp.bfloat16)).astype(jnp.float32)
            return running + position_term, None

        running, _ = lax.scan(add_position, jnp.zeros((D, 2, H), jnp.float32), jnp.arange(CYCLE_LEN, dtype=jnp.int32))
        return running.astype(jnp.bfloat16)

    gradients = lax.map(one_expert, jnp.arange(FLIGHT, dtype=jnp.int32))
    return jnp.transpose(gradients, (1, 0, 2, 3))
```

```python
import functools

import jax
import jax.numpy as jnp
from jax import lax
from jax.experimental import pallas as pl
from jax.experimental.pallas import tpu as pltpu
from jax.sharding import PartitionSpec as P

MESH = pl.DeviceIdType.MESH
CAP = 16
NY, NX, NZ, NC = 8, 4, 4, 2
BF = jnp.bfloat16
F32 = jnp.float32


def dot(a, b):
    return jnp.dot(a, b, preferred_element_type=F32)


def kernel(
    tokens_hbm, routed_hbm, act_hbm, codes_hbm, scales_hbm, out_ref,
    tok, routed, act, codes, scales, codes32, spread, send, recv, relay,
    w, part, other, cot_other, p_t, g, r_a, r_b, f_l, f_r, z_buf,
    in_sem, own_sem, a_send, a_recv, rl_send, rl_recv,
    wz_send, wz_recv, wx_send, wx_recv, ex_send, ex_recv,
    rs_send, rs_recv, z_send, z_recv,
):
    y = lax.axis_index("group")
    b = lax.axis_index("blk")
    x, z, c = b // (NZ * NC), (b // NC) % NZ, b % NC
    half = send.shape[3] - 128
    hid = act.shape[1]

    def blk_of(xx, zz, cc):
        return xx * (NZ * NC) + zz * NC + cc

    right, left, across = (x + 1) % NX, (x + NX - 1) % NX, (x + 2) % NX
    to_right = {"blk": blk_of(right, z, c)}
    to_left = {"blk": blk_of(left, z, c)}
    partner = {"blk": blk_of(x, z, 1 - c)}

    def remote(src, dst, s_sem, r_sem, where):
        return pltpu.make_async_remote_copy(
            src_ref=src, dst_ref=dst, send_sem=s_sem, recv_sem=r_sem,
            device_id=where, device_id_type=MESH,
        )

    loads = [
        pltpu.make_async_copy(codes_hbm, codes, in_sem.at[0]),
        pltpu.make_async_copy(scales_hbm, scales, in_sem.at[1]),
        pltpu.make_async_copy(routed_hbm, routed, in_sem.at[2]),
        pltpu.make_async_copy(tokens_hbm, tok, in_sem.at[3]),
        pltpu.make_async_copy(act_hbm, act, in_sem.at[4]),
    ]
    for load in loads:
        load.start()

    barrier = pltpu.get_barrier_semaphore()
    greeted = 0
    for dy in (1, 2, 3, 5, 6, 7):
        for cc in range(NC):
            pl.semaphore_signal(
                barrier, inc=1,
                device_id={"group": (y + dy) % NY, "blk": blk_of(x, z, cc)},
                device_id_type=MESH,
            )
            greeted += 1
    for where in [partner, to_right, to_left] + [
        {"blk": blk_of(x, (z + k) % NZ, c)} for k in range(1, NZ)
    ]:
        pl.semaphore_signal(barrier, inc=1, device_id=where, device_id_type=MESH)
        greeted += 1

    loads[0].wait()
    loads[1].wait()
    codes32[...] = codes[:, 0].astype(F32)
    sc = scales[0, 0].astype(F32)
    mine_w = z * NX + x
    for j in range(2):
        for q in range(hid // 128):
            piece = codes32[:, j, q * 128:(q + 1) * 128] * sc[j:j + 1, q:q + 1]
            at = q * 256 + j * 128
            w[mine_w, :, at:at + 128] = piece.astype(BF)

    loads[2].wait()
    ids = routed[...]
    lane = lax.broadcasted_iota(jnp.int32, (128, 128), 1)
    row = lax.broadcasted_iota(jnp.int32, (128, 128), 0)
    expert_of, slot_of = lane // CAP, lane % CAP
    hits = [
        jnp.where(ids[:, k:k + 1] == expert_of, 1.0, 0.0) for k in range(ids.shape[1])
    ]
    chosen = functools.reduce(lambda p, q: p + q, hits)
    before = jnp.where(lane < row, 1.0, 0.0).astype(BF)
    position = dot(before, chosen.astype(BF))
    select = jnp.where(position == slot_of.astype(F32), chosen, 0.0)
    for k in range(len(hits)):
        spread[:, k, :] = select * hits[k]
    select_t = select.T.astype(BF)
    pick = spread[...].reshape(128 * len(hits), 128).astype(BF)
    loads[4].wait()
    cot = lax.dot_general(pick, act[...], (((0,), (0,)), ((), ())), preferred_element_type=F32)
    for j in range(NC):
        send[:, j, :, half:half + 128] = (
            cot[:, j * 128:(j + 1) * 128].astype(BF).reshape(NY, CAP, 128)
        )

    pl.semaphore_wait(barrier, greeted)

    wz = []
    for k in range(1, NZ):
        cp = remote(
            w.at[mine_w], w.at[mine_w], wz_send.at[k], wz_recv.at[k],
            {"blk": blk_of(x, (z + k) % NZ, c)},
        )
        cp.start()
        wz.append(cp)

    def wx_copies(k):
        zz = (z + NZ - k) % NZ
        at = zz * NX + x
        return [
            remote(w.at[at], w.at[at], wx_send.at[0, k], wx_recv.at[0, k], to_right),
            remote(w.at[at], w.at[at], wx_send.at[1, k], wx_recv.at[1, k], to_left),
        ]

    def wx_relays(k):
        zz = (z + NZ - k) % NZ
        from_l, from_r = zz * NX + left, zz * NX + right
        top, low = pl.ds(0, 64), pl.ds(64, 64)
        return [
            remote(w.at[from_l, top], w.at[from_l, top], wx_send.at[2, k], wx_recv.at[2, k], to_right),
            remote(w.at[from_r, low], w.at[from_r, low], wx_send.at[3, k], wx_recv.at[3, k], to_left),
        ]

    wx = [wx_copies(k) for k in range(NZ)]
    wr = [wx_relays(k) for k in range(NZ)]
    for cp in wx[0]:
        cp.start()

    loads[3].wait()
    for pair in range(NX * NZ):
        rows = dot(select_t, tok[:, pair * 256:(pair + 1) * 256]).astype(BF)
        at = ((pair % NZ) * NX + pair // NZ) * 128
        for j in range(NC):
            send[:, j, :, at:at + 128] = rows[:, j * 128:(j + 1) * 128].reshape(NY, CAP, 128)

    here = y * NC + c
    first_legs = [
        remote(
            send.at[(y + 4) % NY, j], relay.at[j], rl_send.at[j], rl_recv.at[j],
            {"group": (y + (2 if j == 0 else NY - 2)) % NY},
        )
        for j in range(NC)
    ]
    for cp in first_legs:
        cp.start()
    direct = []
    for n, dy in enumerate((3, 5, 2, 6, 1, 7)):
        to = (y + dy) % NY
        for j in range(NC):
            cp = remote(
                send.at[to, j], recv.at[here], a_send.at[n * NC + j], a_recv.at[here],
                {"group": to, "blk": blk_of(x, z, j)},
            )
            cp.start()
            direct.append(cp)
    own = pltpu.make_async_copy(send.at[y, c], recv.at[here], own_sem)
    own.start()
    cross = remote(send.at[y, 1 - c], recv.at[here], a_send.at[12], a_recv.at[here], partner)
    cross.start()

    for k in range(1, NZ):
        wz[k - 1].wait_recv()
        for cp in wx[k]:
            cp.start()
    second_legs = []
    for j in range(NC):
        first_legs[j].wait_recv()
        source = (y + (NY - 2 if j == 0 else 2)) % NY
        to = (y + (2 if j == 0 else NY - 2)) % NY
        slot = source * NC + c
        cp = remote(
            relay.at[j], recv.at[slot], a_send.at[13 + j], a_recv.at[slot],
            {"group": to, "blk": blk_of(x, z, j)},
        )
        cp.start()
        second_legs.append(cp)
    for k in range(NZ):
        for cp, onward in zip(wx[k], wr[k]):
            cp.wait_recv()
            onward.start()
    for k in range(NZ):
        for cp in wr[k]:
            cp.wait_recv()
    own.wait()
    for n in range(1, NY * NC):
        slot = (here + n) % (NY * NC)
        remote(
            recv.at[slot], recv.at[slot], a_send.at[15], a_recv.at[slot], partner
        ).wait_recv()

    swap_cot = remote(
        recv.at[:, :, pl.ds(half, 128)], cot_other, ex_send.at[2], ex_recv.at[2], partner
    )
    swap_cot.start()
    swaps = []
    rows_here = recv[:, :, :half].reshape(NY * NC * CAP, half)
    for q in range(hid // 128):
        part[q] = dot(rows_here, w[:, :, q * 256:(q + 1) * 256].reshape(half, 256))
        cp = remote(part.at[q], other.at[q], ex_send.at[q], ex_recv.at[q], partner)
        cp.start()
        swaps.append(cp)
    swap_cot.wait_recv()
    for q in range(hid // 128):
        swaps[q].wait_recv()
        gate = part[q, :, :128] + other[q, :, :128]
        up = part[q, :, 128:] + other[q, :, 128:]
        mine = recv[:, :, half:].reshape(NY * NC * CAP, 128).astype(F32)
        theirs = cot_other[...].reshape(NY * NC * CAP, 128).astype(F32)
        cotangent = jnp.where(c == q, mine, theirs)
        s = jax.nn.sigmoid(gate)
        d_gate = cotangent * up * s * (1.0 + gate * (1.0 - s))
        d_up = cotangent * gate * s
        p_t[q * 128:(q + 1) * 128, :] = d_gate.T.astype(BF)
        p_t[hid + q * 128:hid + (q + 1) * 128, :] = d_up.T.astype(BF)

    upper, lower = pl.ds(0, hid), pl.ds(hid, hid)

    def z_of(k):
        return (z + 1 + k) % NZ

    def product(k):
        zz = z_of(k)
        cols = recv[:, :, pl.ds(pl.multiple_of(zz * (NX * 128), 128), NX * 128)].reshape(
            NY * NC * CAP, NX * 128
        )
        for m in range(2):
            got = dot(p_t[m * hid:(m + 1) * hid, :], cols).astype(BF)
            for xx in range(NX):
                g[zz, xx, m * hid:(m + 1) * hid, :] = got[:, xx * 128:(xx + 1) * 128]

    def sends(k):
        zz = z_of(k)
        return [
            remote(g.at[zz, across, upper], r_a.at[zz], rs_send.at[0, k], rs_recv.at[0, k], to_right),
            remote(g.at[zz, across, lower], r_b.at[zz], rs_send.at[1, k], rs_recv.at[1, k], to_left),
            remote(g.at[zz, right, lower], f_l.at[zz, lower], rs_send.at[2, k], rs_recv.at[2, k], to_right),
            remote(g.at[zz, left, upper], f_r.at[zz, upper], rs_send.at[3, k], rs_recv.at[3, k], to_left),
            remote(g.at[zz, right, upper], f_l.at[zz, upper], rs_send.at[4, k], rs_recv.at[4, k], to_right),
            remote(g.at[zz, left, lower], f_r.at[zz, lower], rs_send.at[5, k], rs_recv.at[5, k], to_left),
        ]

    rs = [sends(k) for k in range(NZ)]
    zs = [
        remote(
            g.at[z_of(k), x], z_buf.at[k], z_send.at[k], z_recv.at[k],
            {"blk": blk_of(x, z_of(k), c)},
        )
        for k in range(NZ - 1)
    ]

    def begin(k):
        product(k)
        for cp in rs[k][:4]:
            cp.start()

    def pass_on(k):
        zz = z_of(k)
        rs[k][0].wait_recv()
        g[zz, right, upper] = (g[zz, right, upper].astype(F32) + r_a[zz].astype(F32)).astype(BF)
        rs[k][4].start()
        rs[k][1].wait_recv()
        g[zz, left, lower] = (g[zz, left, lower].astype(F32) + r_b[zz].astype(F32)).astype(BF)
        rs[k][5].start()

    def gathered(k):
        zz = z_of(k)
        for cp in rs[k][2:]:
            cp.wait_recv()
        return g[zz, x].astype(F32) + f_l[zz].astype(F32) + f_r[zz].astype(F32)

    def finish(k):
        g[z_of(k), x] = gathered(k).astype(BF)
        zs[k].start()

    begin(0)
    begin(1)
    for k in range(NZ):
        pass_on(k)
        if k + 2 < NZ:
            begin(k + 2)
        if k >= 1:
            finish(k - 1)
    total = gathered(NZ - 1)
    for k in range(NZ - 1):
        zs[k].wait_recv()
        total = total + z_buf[k].astype(F32)
    out_ref[...] = total.T.astype(BF)

    for cp in wz + direct + first_legs + second_legs + swaps + zs + [swap_cot, cross]:
        cp.wait_send()
    for group in wx + wr + rs:
        for cp in group:
            cp.wait_send()


def local(tokens, routed_experts, act_cotangent, weight_codes, weight_scales):
    rows, width = tokens.shape
    top, hid = act_cotangent.shape[1:]
    half = width // 2
    dma = pltpu.SemaphoreType.DMA
    any_spec = pl.BlockSpec(memory_space=pl.ANY)
    out = pl.pallas_call(
        kernel,
        out_shape=jax.ShapeDtypeStruct((rows, 2 * hid), BF),
        in_specs=[any_spec] * 5,
        out_specs=pl.BlockSpec(memory_space=pltpu.VMEM),
        scratch_shapes=[
            pltpu.VMEM((rows, width), BF),
            pltpu.VMEM((rows, top), jnp.int32),
            pltpu.VMEM((rows * top, hid), BF),
            pltpu.VMEM((rows, 1, 2, hid), BF),
            pltpu.VMEM((1, 1, 2, hid // 128), BF),
            pltpu.VMEM((rows, 2, hid), F32),
            pltpu.VMEM((rows, top, 128), F32),
            pltpu.VMEM((NY, NC, CAP, half + 128), BF),
            pltpu.VMEM((NY * NC, CAP, half + 128), BF),
            pltpu.VMEM((NC, CAP, half + 128), BF),
            pltpu.VMEM((NX * NZ, 128, 2 * hid), BF),
            pltpu.VMEM((2, NY * NC * CAP, hid), F32),
            pltpu.VMEM((2, NY * NC * CAP, hid), F32),
            pltpu.VMEM((NY * NC, CAP, 128), BF),
            pltpu.VMEM((2 * hid, NY * NC * CAP), BF),
            pltpu.VMEM((NZ, NX, 2 * hid, 128), BF),
            pltpu.VMEM((NZ, hid, 128), BF),
            pltpu.VMEM((NZ, hid, 128), BF),
            pltpu.VMEM((NZ, 2 * hid, 128), BF),
            pltpu.VMEM((NZ, 2 * hid, 128), BF),
            pltpu.VMEM((NZ, 2 * hid, 128), BF),
            dma((5,)), dma,
            dma((16,)), dma((16,)), dma((2,)), dma((2,)),
            dma((NZ,)), dma((NZ,)), dma((4, NZ)), dma((4, NZ)),
            dma((3,)), dma((3,)),
            dma((6, NZ)), dma((6, NZ)), dma((NZ,)), dma((NZ,)),
        ],
        compiler_params=pltpu.CompilerParams(
            collective_id=0, has_side_effects=True, vmem_limit_bytes=48 * 1024 * 1024
        ),
    )(tokens, routed_experts, act_cotangent.reshape(rows * top, hid), weight_codes, weight_scales)
    return out.reshape(rows, 1, 2, hid)


def solution(mesh):
    return jax.shard_map(
        local,
        mesh=mesh,
        in_specs=(
            P(("group", "blk"), None),
            P(("group", "blk"), None),
            P(("group", "blk"), None, "att"),
            P("blk", "group", None, "att"),
            P("blk", "group", None, "att"),
        ),
        out_specs=P("blk", "group", None, "att"),
        check_vma=False,
    )
```

```python
import functools

import jax
import jax.numpy as jnp
from jax import lax
from jax.experimental import pallas as pl
from jax.experimental.pallas import tpu as pltpu
from jax.sharding import PartitionSpec as P

MESH = pl.DeviceIdType.MESH
CAP = 16
NY, NX, NZ, NC = 8, 4, 4, 2
BF = jnp.bfloat16
F32 = jnp.float32


def dot(a, b):
    return jnp.dot(a, b, preferred_element_type=F32)


def kernel(
    tokens_hbm, routed_hbm, act_hbm, codes_hbm, scales_hbm, out_ref,
    tok, routed, act, codes, scales, codes32, spread, send, recv, relay,
    w, part, other, cot_other, p_t, g, r_a, r_b, f_l, f_r, z_buf,
    in_sem, own_sem, ready, a_send, a_recv, rl_send, rl_recv,
    wz_send, wz_recv, wx_send, wx_recv, ex_send, ex_recv,
    rs_send, rs_recv, z_send, z_recv,
):
    y = lax.axis_index("group")
    b = lax.axis_index("blk")
    x, z, c = b // (NZ * NC), (b // NC) % NZ, b % NC
    half = send.shape[3] - 128
    hid = act.shape[1]

    def blk_of(xx, zz, cc):
        return xx * (NZ * NC) + zz * NC + cc

    right, left, across = (x + 1) % NX, (x + NX - 1) % NX, (x + 2) % NX
    to_right = {"blk": blk_of(right, z, c)}
    to_left = {"blk": blk_of(left, z, c)}
    partner = {"blk": blk_of(x, z, 1 - c)}

    def remote(src, dst, s_sem, r_sem, where):
        return pltpu.make_async_remote_copy(
            src_ref=src, dst_ref=dst, send_sem=s_sem, recv_sem=r_sem,
            device_id=where, device_id_type=MESH,
        )

    loads = [
        pltpu.make_async_copy(codes_hbm, codes, in_sem.at[0]),
        pltpu.make_async_copy(scales_hbm, scales, in_sem.at[1]),
        pltpu.make_async_copy(routed_hbm, routed, in_sem.at[2]),
        pltpu.make_async_copy(tokens_hbm, tok, in_sem.at[3]),
        pltpu.make_async_copy(act_hbm, act, in_sem.at[4]),
    ]
    for load in loads:
        load.start()

    peers = [(dy, x, z, cc) for dy in (1, 2, 3, 5, 6, 7) for cc in range(NC)]
    peers += [(0, x, z, 1 - c), (0, right, z, c), (0, left, z, c)]
    peers += [(0, x, (z + k) % NZ, c) for k in range(1, NZ)]

    def is_last(dy, xx, zz, cc):
        return ((y + dy) % NY == 0) & (blk_of(xx, zz, cc) == 0)

    def place(dy, xx, zz, cc):
        return {"group": (y + dy) % NY, "blk": blk_of(xx, zz, cc)}

    last = (y == 0) & (b == 0)
    by_last = functools.reduce(lambda p, q: p | q, [is_last(*peer) for peer in peers])
    owed = by_last.astype(jnp.int32)
    barrier = pltpu.get_barrier_semaphore()

    @pl.when(jnp.logical_not(last))
    def _():
        for peer in peers:
            pl.semaphore_signal(barrier, inc=1, device_id=place(*peer), device_id_type=MESH)

    loads[0].wait()
    loads[1].wait()
    codes32[...] = codes[:, 0].astype(F32)
    sc = scales[0, 0].astype(F32)
    mine_w = z * NX + x
    for j in range(2):
        for q in range(hid // 128):
            piece = codes32[:, j, q * 128:(q + 1) * 128] * sc[j:j + 1, q:q + 1]
            at = q * 256 + j * 128
            w[mine_w, :, at:at + 128] = piece.astype(BF)

    loads[2].wait()
    ids = routed[...].T
    lane = lax.broadcasted_iota(jnp.int32, (128, 128), 1)
    row = lax.broadcasted_iota(jnp.int32, (128, 128), 0)
    expert_of, slot_of = lane // CAP, lane % CAP
    hits = [
        jnp.where(ids[:, k:k + 1] == expert_of, 1.0, 0.0) for k in range(ids.shape[1])
    ]
    chosen = functools.reduce(lambda p, q: p + q, hits)
    before = jnp.where(lane < row, 1.0, 0.0).astype(BF)
    position = dot(before, chosen.astype(BF))
    select = jnp.where(position == slot_of.astype(F32), chosen, 0.0)
    for k in range(len(hits)):
        spread[:, k, :] = select * hits[k]
    select_t = select.T.astype(BF)
    pick = spread[...].reshape(128 * len(hits), 128).astype(BF)
    loads[4].wait()
    cot = lax.dot_general(pick, act[...], (((0,), (0,)), ((), ())), preferred_element_type=F32)
    for j in range(NC):
        send[:, j, :, half:half + 128] = (
            cot[:, j * 128:(j + 1) * 128].astype(BF).reshape(NY, CAP, 128)
        )

    pl.semaphore_wait(barrier, len(peers) - owed)

    @pl.when(last)
    def _():
        for peer in peers:
            pl.semaphore_signal(ready, inc=1, device_id=place(*peer), device_id_type=MESH)

    later = []

    def do(waits, starts, touches_last):
        def act():
            for cp in waits:
                cp.wait_recv()
            for cp in starts:
                cp.start()

        pl.when(jnp.logical_not(touches_last))(act)
        later.append((touches_last, act))

    wz, wx, wr = [None], [], []
    for k in range(1, NZ):
        wz.append(remote(
            w.at[mine_w], w.at[mine_w], wz_send.at[k], wz_recv.at[k],
            {"blk": blk_of(x, (z + k) % NZ, c)},
        ))
        do([], [wz[k]], is_last(0, x, (z + k) % NZ, c))
    top, low = pl.ds(0, 64), pl.ds(64, 64)
    for k in range(NZ):
        row_of = ((z + NZ - k) % NZ) * NX
        here_w, left_w, right_w = w.at[row_of + x], w.at[row_of + left], w.at[row_of + right]
        wx.append([
            remote(here_w, here_w, wx_send.at[0, k], wx_recv.at[0, k], to_right),
            remote(here_w, here_w, wx_send.at[1, k], wx_recv.at[1, k], to_left),
        ])
        wr.append([
            remote(left_w.at[top], left_w.at[top], wx_send.at[2, k], wx_recv.at[2, k], to_right),
            remote(right_w.at[low], right_w.at[low], wx_send.at[3, k], wx_recv.at[3, k], to_left),
        ])
    right_last, left_last = is_last(0, right, z, c), is_last(0, left, z, c)
    do([], [wx[0][0]], right_last)
    do([], [wx[0][1]], left_last)

    loads[3].wait()
    for pair in range(NX * NZ):
        rows = dot(select_t, tok[:, pair * 256:(pair + 1) * 256]).astype(BF)
        at = ((pair % NZ) * NX + pair // NZ) * 128
        for j in range(NC):
            send[:, j, :, at:at + 128] = rows[:, j * 128:(j + 1) * 128].reshape(NY, CAP, 128)

    here = y * NC + c
    first_legs, second_legs, direct = [], [], []
    for j in range(NC):
        dy = 2 if j == 0 else NY - 2
        cp = remote(
            send.at[(y + 4) % NY, j], relay.at[j], rl_send.at[j], rl_recv.at[j],
            {"group": (y + dy) % NY},
        )
        first_legs.append(cp)
        do([], [cp], is_last(dy, x, z, c))

    def rows_to(*ways):
        for dy in ways:
            to = (y + dy) % NY
            for j in range(NC):
                cp = remote(
                    send.at[to, j], recv.at[here], a_send.at[len(direct)], a_recv.at[here],
                    {"group": to, "blk": blk_of(x, z, j)},
                )
                direct.append(cp)
                do([], [cp], is_last(dy, x, z, j))

    rows_to(3, 5, 2, 6)
    own = pltpu.make_async_copy(send.at[y, c], recv.at[here], own_sem)
    own.start()

    for k in range(1, NZ):
        late = is_last(0, x, (z + NZ - k) % NZ, c)
        do([wz[k]], [], late)
        do([], [wx[k][0]], late | right_last)
        do([], [wx[k][1]], late | left_last)
    for j in range(NC):
        back, on = (NY - 2, 2) if j == 0 else (2, NY - 2)
        slot = ((y + back) % NY) * NC + c
        cp = remote(
            relay.at[j], recv.at[slot], a_send.at[13 + j], a_recv.at[slot],
            {"group": (y + on) % NY, "blk": blk_of(x, z, j)},
        )
        second_legs.append(cp)
        do([first_legs[j]], [cp], is_last(back, x, z, c) | is_last(on, x, z, j))
    rows_to(1, 7)
    cross = remote(send.at[y, 1 - c], recv.at[here], a_send.at[12], a_recv.at[here], partner)
    do([], [cross], is_last(0, x, z, 1 - c))
    for k in range(NZ):
        for cp, onward in zip(wx[k], wr[k]):
            do([cp], [onward], right_last | left_last)

    @pl.when(by_last)
    def _():
        pl.semaphore_wait(ready, 1)
        for touches_last, act in list(later):
            pl.when(touches_last)(act)

    for k in range(NZ):
        for cp in wr[k]:
            cp.wait_recv()
    own.wait()
    for n in range(1, NY * NC):
        slot = (here + n) % (NY * NC)
        remote(
            recv.at[slot], recv.at[slot], a_send.at[15], a_recv.at[slot], partner
        ).wait_recv()

    swap_cot = remote(
        recv.at[:, :, pl.ds(half, 128)], cot_other, ex_send.at[2], ex_recv.at[2], partner
    )
    swap_cot.start()
    swaps = []
    rows_here = recv[:, :, :half].reshape(NY * NC * CAP, half)
    for q in range(hid // 128):
        part[q] = dot(rows_here, w[:, :, q * 256:(q + 1) * 256].reshape(half, 256))
        cp = remote(part.at[q], other.at[q], ex_send.at[q], ex_recv.at[q], partner)
        cp.start()
        swaps.append(cp)
    swap_cot.wait_recv()
    for q in range(hid // 128):
        swaps[q].wait_recv()
        gate = part[q, :, :128] + other[q, :, :128]
        up = part[q, :, 128:] + other[q, :, 128:]
        mine = recv[:, :, half:].reshape(NY * NC * CAP, 128).astype(F32)
        theirs = cot_other[...].reshape(NY * NC * CAP, 128).astype(F32)
        cotangent = jnp.where(c == q, mine, theirs)
        s = jax.nn.sigmoid(gate)
        d_gate = cotangent * up * s * (1.0 + gate * (1.0 - s))
        d_up = cotangent * gate * s
        p_t[q * 128:(q + 1) * 128, :] = d_gate.T.astype(BF)
        p_t[hid + q * 128:hid + (q + 1) * 128, :] = d_up.T.astype(BF)

    upper, lower = pl.ds(0, hid), pl.ds(hid, hid)

    def z_of(k):
        return (z + 1 + k) % NZ

    def product(k):
        zz = z_of(k)
        cols = recv[:, :, pl.ds(pl.multiple_of(zz * (NX * 128), 128), NX * 128)].reshape(
            NY * NC * CAP, NX * 128
        )
        for m in range(2):
            got = dot(p_t[m * hid:(m + 1) * hid, :], cols).astype(BF)
            for xx in range(NX):
                g[zz, xx, m * hid:(m + 1) * hid, :] = got[:, xx * 128:(xx + 1) * 128]

    def sends(k):
        zz = z_of(k)
        return [
            remote(g.at[zz, across, upper], r_a.at[zz], rs_send.at[0, k], rs_recv.at[0, k], to_right),
            remote(g.at[zz, across, lower], r_b.at[zz], rs_send.at[1, k], rs_recv.at[1, k], to_left),
            remote(g.at[zz, right, lower], f_l.at[zz, lower], rs_send.at[2, k], rs_recv.at[2, k], to_right),
            remote(g.at[zz, left, upper], f_r.at[zz, upper], rs_send.at[3, k], rs_recv.at[3, k], to_left),
            remote(g.at[zz, right, upper], f_l.at[zz, upper], rs_send.at[4, k], rs_recv.at[4, k], to_right),
            remote(g.at[zz, left, lower], f_r.at[zz, lower], rs_send.at[5, k], rs_recv.at[5, k], to_left),
        ]

    rs = [sends(k) for k in range(NZ)]
    zs = [
        remote(
            g.at[z_of(k), x], z_buf.at[k], z_send.at[k], z_recv.at[k],
            {"blk": blk_of(x, z_of(k), c)},
        )
        for k in range(NZ - 1)
    ]

    def begin(k):
        product(k)
        for cp in rs[k][:4]:
            cp.start()

    def pass_on(k):
        zz = z_of(k)
        rs[k][0].wait_recv()
        g[zz, right, upper] = (g[zz, right, upper].astype(F32) + r_a[zz].astype(F32)).astype(BF)
        rs[k][4].start()
        rs[k][1].wait_recv()
        g[zz, left, lower] = (g[zz, left, lower].astype(F32) + r_b[zz].astype(F32)).astype(BF)
        rs[k][5].start()

    def gathered(k):
        zz = z_of(k)
        for cp in rs[k][2:]:
            cp.wait_recv()
        return g[zz, x].astype(F32) + f_l[zz].astype(F32) + f_r[zz].astype(F32)

    def finish(k):
        g[z_of(k), x] = gathered(k).astype(BF)
        zs[k].start()

    begin(0)
    begin(1)
    for k in range(NZ):
        pass_on(k)
        if k + 2 < NZ:
            begin(k + 2)
        if k >= 1:
            finish(k - 1)
    total = gathered(NZ - 1)
    for k in range(NZ - 1):
        zs[k].wait_recv()
        total = total + z_buf[k].astype(F32)
    out_ref[...] = total.T.astype(BF)

    for cp in wz[1:] + direct + first_legs + second_legs + swaps + zs + [swap_cot, cross]:
        cp.wait_send()
    for group in wx + wr + rs:
        for cp in group:
            cp.wait_send()


def local(tokens, routed_experts, act_cotangent, weight_codes, weight_scales):
    rows, width = tokens.shape
    top, hid = act_cotangent.shape[1:]
    half = width // 2
    dma = pltpu.SemaphoreType.DMA
    hbm = pl.BlockSpec(memory_space=pltpu.HBM)
    out = pl.pallas_call(
        kernel,
        out_shape=jax.ShapeDtypeStruct((rows, 2 * hid), BF),
        in_specs=[hbm] * 5,
        out_specs=pl.BlockSpec(memory_space=pltpu.VMEM),
        scratch_shapes=[
            pltpu.VMEM((rows, width), BF),
            pltpu.VMEM((top, rows), jnp.int32),
            pltpu.VMEM((rows * top, hid), BF),
            pltpu.VMEM((rows, 1, 2, hid), BF),
            pltpu.VMEM((1, 1, 2, hid // 128), BF),
            pltpu.VMEM((rows, 2, hid), F32),
            pltpu.VMEM((rows, top, 128), F32),
            pltpu.VMEM((NY, NC, CAP, half + 128), BF),
            pltpu.VMEM((NY * NC, CAP, half + 128), BF),
            pltpu.VMEM((NC, CAP, half + 128), BF),
            pltpu.VMEM((NX * NZ, 128, 2 * hid), BF),
            pltpu.VMEM((2, NY * NC * CAP, hid), F32),
            pltpu.VMEM((2, NY * NC * CAP, hid), F32),
            pltpu.VMEM((NY * NC, CAP, 128), BF),
            pltpu.VMEM((2 * hid, NY * NC * CAP), BF),
            pltpu.VMEM((NZ, NX, 2 * hid, 128), BF),
            pltpu.VMEM((NZ, hid, 128), BF),
            pltpu.VMEM((NZ, hid, 128), BF),
            pltpu.VMEM((NZ, 2 * hid, 128), BF),
            pltpu.VMEM((NZ, 2 * hid, 128), BF),
            pltpu.VMEM((NZ, 2 * hid, 128), BF),
            dma((5,)), dma, pltpu.SemaphoreType.REGULAR,
            dma((16,)), dma((16,)), dma((2,)), dma((2,)),
            dma((NZ,)), dma((NZ,)), dma((4, NZ)), dma((4, NZ)),
            dma((3,)), dma((3,)),
            dma((6, NZ)), dma((6, NZ)), dma((NZ,)), dma((NZ,)),
        ],
        compiler_params=pltpu.CompilerParams(
            collective_id=0, has_side_effects=True, vmem_limit_bytes=48 * 1024 * 1024
        ),
    )(*[
        pltpu.with_memory_space_constraint(a, pltpu.HBM)
        for a in (
            tokens, routed_experts.T, act_cotangent.reshape(rows * top, hid),
            weight_codes, weight_scales,
        )
    ])
    return out.reshape(rows, 1, 2, hid)


def solution(mesh):
    return jax.shard_map(
        local,
        mesh=mesh,
        in_specs=(
            P(("group", "blk"), None),
            P(("group", "blk"), None),
            P(("group", "blk"), None, "att"),
            P("blk", "group", None, "att"),
            P("blk", "group", None, "att"),
        ),
        out_specs=P("blk", "group", None, "att"),
        check_vma=False,
    )
```

```python
import functools

import jax
import jax.numpy as jnp
from jax import lax
from jax.experimental import pallas as pl
from jax.experimental.pallas import tpu as pltpu
from jax.sharding import PartitionSpec as P

MESH = pl.DeviceIdType.MESH
CAP = 16
NY, NX, NZ, NC = 8, 4, 4, 2
BF = jnp.bfloat16
F32 = jnp.float32


def dot(a, b):
    return jnp.dot(a, b, preferred_element_type=F32)


def kernel(
    tokens_hbm, routed_hbm, act_hbm, codes_hbm, scales_hbm, out_ref,
    tok, routed, act, codes, scales, codes32, spread, send, recv, relay,
    w, part, other, cot_other, p_t, g, r_a, r_b, f_l, f_r, z_buf,
    in_sem, own_sem, ready, a_send, a_recv, rl_send, rl_recv,
    wz_send, wz_recv, wx_send, wx_recv, ex_send, ex_recv,
    rs_send, rs_recv, z_send, z_recv,
):
    y = lax.axis_index("group")
    b = lax.axis_index("blk")
    x, z, c = b // (NZ * NC), (b // NC) % NZ, b % NC
    half = send.shape[3] - 128
    hid = act.shape[1]

    def blk_of(xx, zz, cc):
        return xx * (NZ * NC) + zz * NC + cc

    right, left, across = (x + 1) % NX, (x + NX - 1) % NX, (x + 2) % NX
    z_near = [z, z + 1 - 2 * (z % 2), 2 - z // 2, 3 - 3 * (z // 2)]
    to_right = {"blk": blk_of(right, z, c)}
    to_left = {"blk": blk_of(left, z, c)}
    partner = {"blk": blk_of(x, z, 1 - c)}

    def remote(src, dst, s_sem, r_sem, where):
        return pltpu.make_async_remote_copy(
            src_ref=src, dst_ref=dst, send_sem=s_sem, recv_sem=r_sem,
            device_id=where, device_id_type=MESH,
        )

    loads = [
        pltpu.make_async_copy(codes_hbm, codes, in_sem.at[0]),
        pltpu.make_async_copy(scales_hbm, scales, in_sem.at[1]),
        pltpu.make_async_copy(routed_hbm, routed, in_sem.at[2]),
        pltpu.make_async_copy(tokens_hbm, tok, in_sem.at[3]),
        pltpu.make_async_copy(act_hbm, act, in_sem.at[4]),
    ]
    for load in loads:
        load.start()

    peers = [(dy, x, z, cc) for dy in (1, 2, 3, 5, 6, 7) for cc in range(NC)]
    peers += [(0, x, z, 1 - c), (0, right, z, c), (0, left, z, c)]
    peers += [(0, x, (z + k) % NZ, c) for k in range(1, NZ)]

    def is_last(dy, xx, zz, cc):
        return ((y + dy) % NY == 0) & (blk_of(xx, zz, cc) == 0) & (lax.axis_index("att") == 0)

    def place(dy, xx, zz, cc):
        return {"group": (y + dy) % NY, "blk": blk_of(xx, zz, cc)}

    last = is_last(0, x, z, c)
    by_last = functools.reduce(lambda p, q: p | q, [is_last(*peer) for peer in peers])
    owed = by_last.astype(jnp.int32)
    barrier = pltpu.get_barrier_semaphore()

    @pl.when(jnp.logical_not(last))
    def _():
        for peer in peers:
            pl.semaphore_signal(barrier, inc=1, device_id=place(*peer), device_id_type=MESH)

    @pl.when(last)
    def _():
        pl.semaphore_wait(barrier, len(peers))
        for peer in peers:
            pl.semaphore_signal(ready, inc=1, device_id=place(*peer), device_id_type=MESH)

    loads[0].wait()
    loads[1].wait()
    codes32[...] = codes[:, 0].astype(F32)
    sc = scales[0, 0].astype(F32)
    mine_w = z * NX + x
    for j in range(2):
        for q in range(hid // 128):
            piece = codes32[:, j, q * 128:(q + 1) * 128] * sc[j:j + 1, q:q + 1]
            at = q * 256 + j * 128
            w[mine_w, :, at:at + 128] = piece.astype(BF)

    top, low = pl.ds(0, 64), pl.ds(64, 64)
    wz, wx, wr = [None], [], []
    for k in range(NZ):
        row_of = z_near[k] * NX
        here_w, left_w, right_w = w.at[row_of + x], w.at[row_of + left], w.at[row_of + right]
        if k:
            wz.append(remote(
                w.at[mine_w], w.at[mine_w], wz_send.at[k], wz_recv.at[z],
                {"blk": blk_of(x, z_near[k], c)},
            ))
        wx.append([
            remote(here_w, here_w, wx_send.at[0, k], wx_recv.at[0, k], to_right),
            remote(here_w, here_w, wx_send.at[1, k], wx_recv.at[1, k], to_left),
        ])
        wr.append([
            remote(left_w.at[top], left_w.at[top], wx_send.at[2, k], wx_recv.at[2, k], to_right),
            remote(right_w.at[low], right_w.at[low], wx_send.at[3, k], wx_recv.at[3, k], to_left),
        ])

    @pl.when(last)
    def _():
        for cp in wz[1:] + wx[0]:
            cp.start()

    loads[2].wait()
    ids = routed[...].T
    lane = lax.broadcasted_iota(jnp.int32, (128, 128), 1)
    row = lax.broadcasted_iota(jnp.int32, (128, 128), 0)
    expert_of, slot_of = lane // CAP, lane % CAP
    hits = [
        jnp.where(ids[:, k:k + 1] == expert_of, 1.0, 0.0) for k in range(ids.shape[1])
    ]
    chosen = functools.reduce(lambda p, q: p + q, hits)
    before = jnp.where(lane < row, 1.0, 0.0).astype(BF)
    position = dot(before, chosen.astype(BF))
    select = jnp.where(position == slot_of.astype(F32), chosen, 0.0)
    for k in range(len(hits)):
        spread[:, k, :] = select * hits[k]
    select_t = select.T.astype(BF)
    pick = spread[...].reshape(128 * len(hits), 128).astype(BF)
    loads[4].wait()
    cot = lax.dot_general(pick, act[...], (((0,), (0,)), ((), ())), preferred_element_type=F32)
    for j in range(NC):
        send[:, j, :, half:half + 128] = (
            cot[:, j * 128:(j + 1) * 128].astype(BF).reshape(NY, CAP, 128)
        )

    @pl.when(jnp.logical_not(last))
    def _():
        pl.semaphore_wait(barrier, len(peers) - owed)

    later_to, later_from, no = [], [], jnp.logical_not

    def do(waits, starts, to_last, from_last=None):
        def act():
            for cp in waits:
                cp.wait_recv()
            for cp in starts:
                cp.start()

        if from_last is None:
            pl.when(no(to_last))(act)
            later_to.append(([to_last], act))
        elif to_last is None:
            pl.when(no(from_last))(act)
            later_from.append(([from_last], act))
        else:
            pl.when(no(to_last) & no(from_last))(act)
            later_to.append(([to_last, no(from_last)], act))
            later_from.append(([from_last], act))

    right_last, left_last = is_last(0, right, z, c), is_last(0, left, z, c)

    near_last = [is_last(0, x, zz, c) for zz in z_near]

    @pl.when(jnp.logical_not(last))
    def _():
        for k in range(1, NZ):
            do([], [wz[k]], near_last[k])
        do([], [wx[0][0]], right_last)
        do([], [wx[0][1]], left_last)

    loads[3].wait()
    for pair in range(NX * NZ):
        rows = dot(select_t, tok[:, pair * 256:(pair + 1) * 256]).astype(BF)
        at = ((pair % NZ) * NX + pair // NZ) * 128
        for j in range(NC):
            send[:, j, :, at:at + 128] = rows[:, j * 128:(j + 1) * 128].reshape(NY, CAP, 128)

    here = y * NC + c
    first_legs, second_legs, direct = [], [], []
    for j in range(NC):
        dy = 2 if j == 0 else NY - 2
        cp = remote(
            send.at[(y + 4) % NY, j], relay.at[j], rl_send.at[j], rl_recv.at[j],
            {"group": (y + dy) % NY},
        )
        first_legs.append(cp)
        do([], [cp], is_last(dy, x, z, c))

    def rows_to(dy):
        to = (y + dy) % NY
        for j in range(NC):
            direct.append(remote(
                send.at[to, j], recv.at[here], a_send.at[len(direct)], a_recv.at[here],
                {"group": to, "blk": blk_of(x, z, j)},
            ))
        return direct[-NC:]

    for dy in (3, 5, 2, 6):
        for j, cp in enumerate(rows_to(dy)):
            do([], [cp], is_last(dy, x, z, j))
    own = pltpu.make_async_copy(send.at[y, c], recv.at[here], own_sem)
    own.start()

    for k in range(1, NZ):
        late = near_last[k]
        near_w = w.at[z_near[k] * NX + x]
        do([remote(near_w, near_w, wz_send.at[k], wz_recv.at[z_near[k]], partner)], [], None, late)
        do([], [wx[k][0]], right_last, late)
        do([], [wx[k][1]], left_last, late)
    do([wx[0][0]], [wr[0][0]], right_last, left_last)
    do([wx[0][1]], [wr[0][1]], left_last, right_last)

    @pl.when(by_last)
    def _():
        pl.semaphore_wait(ready, 1)
        for flags, act in later_to + later_from:
            pl.when(functools.reduce(lambda p, q: p & q, flags))(act)

    for j in range(NC):
        back, on = (NY - 2, 2) if j == 0 else (2, NY - 2)
        slot = ((y + back) % NY) * NC + c
        cp = remote(
            relay.at[j], recv.at[slot], a_send.at[13 + j], a_recv.at[slot],
            {"group": (y + on) % NY, "blk": blk_of(x, z, j)},
        )
        second_legs.append(cp)
        first_legs[j].wait_recv()
        cp.start()
    for dy in (1, 7):
        for cp in rows_to(dy):
            cp.start()
    cross = remote(send.at[y, 1 - c], recv.at[here], a_send.at[12], a_recv.at[here], partner)
    cross.start()
    for k in range(1, NZ):
        for cp, onward in zip(wx[k], wr[k]):
            cp.wait_recv()
            onward.start()
    for k in range(NZ):
        for cp in wr[k]:
            cp.wait_recv()
    own.wait()
    for n in range(1, NY * NC):
        slot = (here + n) % (NY * NC)
        remote(
            recv.at[slot], recv.at[slot], a_send.at[15], a_recv.at[slot], partner
        ).wait_recv()

    swap_cot = remote(
        recv.at[:, :, pl.ds(half, 128)], cot_other, ex_send.at[2], ex_recv.at[2], partner
    )
    swap_cot.start()
    swaps = []
    rows_here = recv[:, :, :half].reshape(NY * NC * CAP, half)
    for q in range(hid // 128):
        part[q] = dot(rows_here, w[:, :, q * 256:(q + 1) * 256].reshape(half, 256))
        cp = remote(part.at[q], other.at[q], ex_send.at[q], ex_recv.at[q], partner)
        cp.start()
        swaps.append(cp)
    swap_cot.wait_recv()
    for q in range(hid // 128):
        swaps[q].wait_recv()
        gate = part[q, :, :128] + other[q, :, :128]
        up = part[q, :, 128:] + other[q, :, 128:]
        mine = recv[:, :, half:].reshape(NY * NC * CAP, 128).astype(F32)
        theirs = cot_other[...].reshape(NY * NC * CAP, 128).astype(F32)
        cotangent = jnp.where(c == q, mine, theirs)
        s = jax.nn.sigmoid(gate)
        d_gate = cotangent * up * s * (1.0 + gate * (1.0 - s))
        d_up = cotangent * gate * s
        p_t[q * 128:(q + 1) * 128, :] = d_gate.T.astype(BF)
        p_t[hid + q * 128:hid + (q + 1) * 128, :] = d_up.T.astype(BF)

    upper, lower = pl.ds(0, hid), pl.ds(hid, hid)

    def z_of(k):
        return z_near[NZ - 1 - k]

    def product(k):
        zz = z_of(k)
        cols = recv[:, :, pl.ds(pl.multiple_of(zz * (NX * 128), 128), NX * 128)].reshape(
            NY * NC * CAP, NX * 128
        )
        for m in range(2):
            got = dot(p_t[m * hid:(m + 1) * hid, :], cols).astype(BF)
            for xx in range(NX):
                g[zz, xx, m * hid:(m + 1) * hid, :] = got[:, xx * 128:(xx + 1) * 128]

    def sends(k):
        zz = z_of(k)
        return [
            remote(g.at[zz, across, upper], r_a.at[zz], rs_send.at[0, k], rs_recv.at[0, k], to_right),
            remote(g.at[zz, across, lower], r_b.at[zz], rs_send.at[1, k], rs_recv.at[1, k], to_left),
            remote(g.at[zz, right, lower], f_l.at[zz, lower], rs_send.at[2, k], rs_recv.at[2, k], to_right),
            remote(g.at[zz, left, upper], f_r.at[zz, upper], rs_send.at[3, k], rs_recv.at[3, k], to_left),
            remote(g.at[zz, right, upper], f_l.at[zz, upper], rs_send.at[4, k], rs_recv.at[4, k], to_right),
            remote(g.at[zz, left, lower], f_r.at[zz, lower], rs_send.at[5, k], rs_recv.at[5, k], to_left),
        ]

    rs = [sends(k) for k in range(NZ)]
    zs = [
        remote(
            g.at[z_of(k), x], z_buf.at[z], z_send.at[k], z_recv.at[z],
            {"blk": blk_of(x, z_of(k), c)},
        )
        for k in range(NZ - 1)
    ]

    def far_start(k):
        product(k)
        for cp in rs[k][:2]:
            cp.start()

    def near_start(k):
        for cp in rs[k][2:4]:
            cp.start()

    def pass_on(k):
        zz = z_of(k)
        rs[k][0].wait_recv()
        g[zz, right, upper] = (g[zz, right, upper].astype(F32) + r_a[zz].astype(F32)).astype(BF)
        rs[k][4].start()
        rs[k][1].wait_recv()
        g[zz, left, lower] = (g[zz, left, lower].astype(F32) + r_b[zz].astype(F32)).astype(BF)
        rs[k][5].start()

    def gathered(k):
        zz = z_of(k)
        for cp in rs[k][2:]:
            cp.wait_recv()
        return g[zz, x].astype(F32) + f_l[zz].astype(F32) + f_r[zz].astype(F32)

    def finish(k):
        g[z_of(k), x] = gathered(k).astype(BF)
        zs[k].start()

    far_start(0)
    far_start(1)
    near_start(0)
    near_start(1)
    far_start(2)
    pass_on(0)
    near_start(2)
    pass_on(1)
    product(3)
    pass_on(2)
    finish(0)
    for cp in rs[3][:4]:
        cp.start()
    finish(1)
    finish(2)
    pass_on(3)
    total = gathered(NZ - 1)
    for k in range(1, NZ):
        got = z_buf.at[z_near[k]]
        remote(got, got, z_send.at[k], z_recv.at[z_near[k]], partner).wait_recv()
        total = total + got[...].astype(F32)
    out_ref[...] = total.T.astype(BF)

    for cp in wz[1:] + direct + first_legs + second_legs + swaps + zs + [swap_cot, cross]:
        cp.wait_send()
    for group in wx + wr + rs:
        for cp in group:
            cp.wait_send()


def local(tokens, routed_experts, act_cotangent, weight_codes, weight_scales):
    rows, width = tokens.shape
    top, hid = act_cotangent.shape[1:]
    half = width // 2
    dma = pltpu.SemaphoreType.DMA
    hbm = pl.BlockSpec(memory_space=pltpu.HBM)
    out = pl.pallas_call(
        kernel,
        out_shape=jax.ShapeDtypeStruct((rows, 2 * hid), BF),
        in_specs=[hbm] * 5,
        out_specs=pl.BlockSpec(memory_space=pltpu.VMEM),
        scratch_shapes=[
            pltpu.VMEM((rows, width), BF),
            pltpu.VMEM((top, rows), jnp.int32),
            pltpu.VMEM((rows * top, hid), BF),
            pltpu.VMEM((rows, 1, 2, hid), BF),
            pltpu.VMEM((1, 1, 2, hid // 128), BF),
            pltpu.VMEM((rows, 2, hid), F32),
            pltpu.VMEM((rows, top, 128), F32),
            pltpu.VMEM((NY, NC, CAP, half + 128), BF),
            pltpu.VMEM((NY * NC, CAP, half + 128), BF),
            pltpu.VMEM((NC, CAP, half + 128), BF),
            pltpu.VMEM((NX * NZ, 128, 2 * hid), BF),
            pltpu.VMEM((2, NY * NC * CAP, hid), F32),
            pltpu.VMEM((2, NY * NC * CAP, hid), F32),
            pltpu.VMEM((NY * NC, CAP, 128), BF),
            pltpu.VMEM((2 * hid, NY * NC * CAP), BF),
            pltpu.VMEM((NZ, NX, 2 * hid, 128), BF),
            pltpu.VMEM((NZ, hid, 128), BF),
            pltpu.VMEM((NZ, hid, 128), BF),
            pltpu.VMEM((NZ, 2 * hid, 128), BF),
            pltpu.VMEM((NZ, 2 * hid, 128), BF),
            pltpu.VMEM((NZ, 2 * hid, 128), BF),
            dma((5,)), dma, pltpu.SemaphoreType.REGULAR,
            dma((16,)), dma((16,)), dma((2,)), dma((2,)),
            dma((NZ,)), dma((NZ,)), dma((4, NZ)), dma((4, NZ)),
            dma((3,)), dma((3,)),
            dma((6, NZ)), dma((6, NZ)), dma((NZ,)), dma((NZ,)),
        ],
        compiler_params=pltpu.CompilerParams(
            collective_id=0, has_side_effects=True, vmem_limit_bytes=48 * 1024 * 1024
        ),
    )(*[
        pltpu.with_memory_space_constraint(a, pltpu.HBM)
        for a in (
            tokens, routed_experts.T, act_cotangent.reshape(rows * top, hid),
            weight_codes, weight_scales,
        )
    ])
    return out.reshape(rows, 1, 2, hid)


def solution(mesh):
    return jax.shard_map(
        local,
        mesh=mesh,
        in_specs=(
            P(("group", "blk"), None),
            P(("group", "blk"), None),
            P(("group", "blk"), None, "att"),
            P("blk", "group", None, "att"),
            P("blk", "group", None, "att"),
        ),
        out_specs=P("blk", "group", None, "att"),
        check_vma=False,
    )
```

```python
import functools

import jax
import jax.numpy as jnp
from jax import lax
from jax.experimental import pallas as pl
from jax.experimental.pallas import tpu as pltpu
from jax.sharding import PartitionSpec as P

MESH = pl.DeviceIdType.MESH
CAP = 16
NY, NX, NZ, NC = 8, 4, 4, 2
BF = jnp.bfloat16
F32 = jnp.float32


def dot(a, b):
    return jnp.dot(a, b, preferred_element_type=F32)


def kernel(
    tokens_hbm, routed_hbm, act_hbm, codes_hbm, scales_hbm, out_ref,
    tok, routed, act, codes, scales, codes32, spread, send, recv, relay,
    w, part, part_sent, other, cot_other, p_t, g, r_a, r_b, f_l, f_r, z_buf,
    in_sem, own_sem, ready, a_send, a_recv, rl_send, rl_recv,
    wz_send, wz_recv, wx_send, wx_recv, ex_send, ex_recv,
    rs_send, rs_recv, z_send, z_recv,
):
    y = lax.axis_index("group")
    b = lax.axis_index("blk")
    x, z, c = b // (NZ * NC), (b // NC) % NZ, b % NC
    half = send.shape[3] - 128
    hid = act.shape[1]

    def blk_of(xx, zz, cc):
        return xx * (NZ * NC) + zz * NC + cc

    right, left, across = (x + 1) % NX, (x + NX - 1) % NX, (x + 2) % NX
    z_near = [z, z + 1 - 2 * (z % 2), 2 - z // 2, 3 - 3 * (z // 2)]
    to_right = {"blk": blk_of(right, z, c)}
    to_left = {"blk": blk_of(left, z, c)}
    partner = {"blk": blk_of(x, z, 1 - c)}

    def remote(src, dst, s_sem, r_sem, where):
        return pltpu.make_async_remote_copy(
            src_ref=src, dst_ref=dst, send_sem=s_sem, recv_sem=r_sem,
            device_id=where, device_id_type=MESH,
        )

    loads = [
        pltpu.make_async_copy(codes_hbm, codes, in_sem.at[0]),
        pltpu.make_async_copy(scales_hbm, scales, in_sem.at[1]),
        pltpu.make_async_copy(routed_hbm, routed, in_sem.at[2]),
        pltpu.make_async_copy(tokens_hbm, tok, in_sem.at[3]),
        pltpu.make_async_copy(act_hbm, act, in_sem.at[4]),
    ]
    for load in loads:
        load.start()

    peers = [(dy, x, z, cc) for dy in (1, 2, 3, 5, 6, 7) for cc in range(NC)]
    peers += [(0, x, z, 1 - c), (0, right, z, c), (0, left, z, c)]
    peers += [(0, x, (z + k) % NZ, c) for k in range(1, NZ)]

    def is_last(dy, xx, zz, cc):
        return ((y + dy) % NY == 0) & (blk_of(xx, zz, cc) == 0) & (lax.axis_index("att") == 0)

    def place(dy, xx, zz, cc):
        return {"group": (y + dy) % NY, "blk": blk_of(xx, zz, cc)}

    last = is_last(0, x, z, c)
    by_last = functools.reduce(lambda p, q: p | q, [is_last(*peer) for peer in peers])
    owed = by_last.astype(jnp.int32)
    barrier = pltpu.get_barrier_semaphore()

    @pl.when(jnp.logical_not(last))
    def _():
        for peer in peers:
            pl.semaphore_signal(barrier, inc=1, device_id=place(*peer), device_id_type=MESH)

    @pl.when(last)
    def _():
        pl.semaphore_wait(barrier, len(peers))
        for peer in peers:
            pl.semaphore_signal(ready, inc=1, device_id=place(*peer), device_id_type=MESH)

    loads[0].wait()
    loads[1].wait()
    codes32[...] = codes[:, 0].astype(F32)
    sc = scales[0, 0].astype(F32)
    mine_w = z * NX + x
    for j in range(2):
        for q in range(hid // 128):
            piece = codes32[:, j, q * 128:(q + 1) * 128] * sc[j:j + 1, q:q + 1]
            at = q * 256 + j * 128
            w[mine_w, :, at:at + 128] = piece.astype(BF)

    top, low = pl.ds(0, 64), pl.ds(64, 64)
    wz, wx, wr = [None], [], []
    for k in range(NZ):
        row_of = z_near[k] * NX
        here_w, left_w, right_w = w.at[row_of + x], w.at[row_of + left], w.at[row_of + right]
        if k:
            wz.append(remote(
                w.at[mine_w], w.at[mine_w], wz_send.at[k], wz_recv.at[z],
                {"blk": blk_of(x, z_near[k], c)},
            ))
        wx.append([
            remote(here_w, here_w, wx_send.at[0, k], wx_recv.at[0, k], to_right),
            remote(here_w, here_w, wx_send.at[1, k], wx_recv.at[1, k], to_left),
        ])
        wr.append([
            remote(left_w.at[top], left_w.at[top], wx_send.at[2, k], wx_recv.at[2, k], to_right),
            remote(right_w.at[low], right_w.at[low], wx_send.at[3, k], wx_recv.at[3, k], to_left),
        ])

    @pl.when(last)
    def _():
        for cp in wz[1:] + wx[0]:
            cp.start()

    loads[2].wait()
    ids = routed[...].T
    lane = lax.broadcasted_iota(jnp.int32, (128, 128), 1)
    row = lax.broadcasted_iota(jnp.int32, (128, 128), 0)
    expert_of, slot_of = lane // CAP, lane % CAP
    hits = [
        jnp.where(ids[:, k:k + 1] == expert_of, 1.0, 0.0) for k in range(ids.shape[1])
    ]
    chosen = functools.reduce(lambda p, q: p + q, hits)
    before = jnp.where(lane < row, 1.0, 0.0).astype(BF)
    position = dot(before, chosen.astype(BF))
    select = jnp.where(position == slot_of.astype(F32), chosen, 0.0)
    for k in range(len(hits)):
        spread[:, k, :] = select * hits[k]
    select_t = select.T.astype(BF)
    pick = spread[...].reshape(128 * len(hits), 128).astype(BF)
    loads[4].wait()
    cot = lax.dot_general(pick, act[...], (((0,), (0,)), ((), ())), preferred_element_type=F32)
    for j in range(NC):
        send[:, j, :, half:half + 128] = (
            cot[:, j * 128:(j + 1) * 128].astype(BF).reshape(NY, CAP, 128)
        )

    @pl.when(jnp.logical_not(last))
    def _():
        pl.semaphore_wait(barrier, len(peers) - owed)

    later_to, later_from, no = [], [], jnp.logical_not

    def do(waits, starts, to_last, from_last=None):
        def act():
            for cp in waits:
                cp.wait_recv()
            for cp in starts:
                cp.start()

        if from_last is None:
            pl.when(no(to_last))(act)
            later_to.append(([to_last], act))
        elif to_last is None:
            pl.when(no(from_last))(act)
            later_from.append(([from_last], act))
        else:
            pl.when(no(to_last) & no(from_last))(act)
            later_to.append(([to_last, no(from_last)], act))
            later_from.append(([from_last], act))

    right_last, left_last = is_last(0, right, z, c), is_last(0, left, z, c)

    near_last = [is_last(0, x, zz, c) for zz in z_near]

    @pl.when(jnp.logical_not(last))
    def _():
        for k in range(1, NZ):
            do([], [wz[k]], near_last[k])
        do([], [wx[0][0]], right_last)
        do([], [wx[0][1]], left_last)

    loads[3].wait()
    for pair in range(NX * NZ):
        rows = dot(select_t, tok[:, pair * 256:(pair + 1) * 256]).astype(BF)
        at = ((pair % NZ) * NX + pair // NZ) * 128
        for j in range(NC):
            send[:, j, :, at:at + 128] = rows[:, j * 128:(j + 1) * 128].reshape(NY, CAP, 128)

    here = y * NC + c
    first_legs, second_legs, direct = [], [], []
    for j in range(NC):
        dy = 2 if j == 0 else NY - 2
        cp = remote(
            send.at[(y + 4) % NY, j], relay.at[j], rl_send.at[j], rl_recv.at[j],
            {"group": (y + dy) % NY},
        )
        first_legs.append(cp)
        do([], [cp], is_last(dy, x, z, c))

    def rows_to(dy):
        to = (y + dy) % NY
        for j in range(NC):
            direct.append(remote(
                send.at[to, j], recv.at[here], a_send.at[len(direct)], a_recv.at[here],
                {"group": to, "blk": blk_of(x, z, j)},
            ))
        return direct[-NC:]

    for dy in (3, 5):
        for j, cp in enumerate(rows_to(dy)):
            do([], [cp], is_last(dy, x, z, j))
    own = pltpu.make_async_copy(send.at[y, c], recv.at[here], own_sem)
    own.start()

    def z_rows(k):
        near_w = w.at[z_near[k] * NX + x]
        return remote(near_w, near_w, wz_send.at[k], wz_recv.at[z_near[k]], partner)

    def pass_z(k):
        z_rows(k).wait_recv()
        for cp in wx[k]:
            cp.start()

    def pass_half(k):
        for cp, onward in zip(wx[k], wr[k]):
            cp.wait_recv()
            onward.start()

    do([z_rows(1)], [], None, near_last[1])
    do([], [wx[1][0]], right_last, near_last[1])
    do([], [wx[1][1]], left_last, near_last[1])

    @pl.when(by_last)
    def _():
        pl.semaphore_wait(ready, 1)
        for flags, act in later_to:
            pl.when(functools.reduce(lambda p, q: p & q, flags))(act)

    held = []
    for j in range(NC):
        back, on = (NY - 2, 2) if j == 0 else (2, NY - 2)
        slot = ((y + back) % NY) * NC + c
        second_legs.append(remote(
            relay.at[j], recv.at[slot], a_send.at[13 + j], a_recv.at[slot],
            {"group": (y + on) % NY, "blk": blk_of(x, z, j)},
        ))
        held.append(last | is_last(back, x, z, c))

    def pass_rows(j):
        first_legs[j].wait_recv()
        second_legs[j].start()

    for dy in (2, 6):
        for cp in rows_to(dy):
            cp.start()
    for j in range(NC):
        pl.when(no(held[j]))(functools.partial(pass_rows, j))
    for dy in (1, 7):
        for cp in rows_to(dy):
            cp.start()
    cross = remote(send.at[y, 1 - c], recv.at[here], a_send.at[12], a_recv.at[here], partner)
    cross.start()
    pass_z(2)
    pass_half(0)
    pass_z(3)

    @pl.when(by_last)
    def _():
        for flags, act in later_from:
            pl.when(functools.reduce(lambda p, q: p & q, flags))(act)

    pass_half(1)
    for j in range(NC):
        pl.when(held[j])(functools.partial(pass_rows, j))
    pass_half(2)
    pass_half(3)
    for k in range(NZ):
        for cp in wr[k]:
            cp.wait_recv()
    own.wait()
    for n in range(1, NY * NC):
        slot = (here + n) % (NY * NC)
        remote(
            recv.at[slot], recv.at[slot], a_send.at[15], a_recv.at[slot], partner
        ).wait_recv()

    swap_cot = remote(
        recv.at[:, :, pl.ds(half, 128)], cot_other, ex_send.at[2], ex_recv.at[2], partner
    )
    swap_cot.start()
    swaps = []
    rows_here = recv[:, :, :half].reshape(NY * NC * CAP, half)
    for q in range(hid // 128):
        part[q] = dot(rows_here, w[:, :, q * 256:(q + 1) * 256].reshape(half, 256))
        part_sent[q] = part[q].astype(BF)
        cp = remote(part_sent.at[q], other.at[q], ex_send.at[q], ex_recv.at[q], partner)
        cp.start()
        swaps.append(cp)

    def backward(q):
        swaps[q].wait_recv()
        gate = part[q, :, :128] + other[q, :, :128].astype(F32)
        up = part[q, :, 128:] + other[q, :, 128:].astype(F32)
        mine = recv[:, :, half:].reshape(NY * NC * CAP, 128).astype(F32)
        theirs = cot_other[...].reshape(NY * NC * CAP, 128).astype(F32)
        cotangent = jnp.where(c == q, mine, theirs)
        s = jax.nn.sigmoid(gate)
        d_gate = cotangent * up * s * (1.0 + gate * (1.0 - s))
        d_up = cotangent * gate * s
        p_t[q * 256:q * 256 + 128, :] = d_gate.T.astype(BF)
        p_t[q * 256 + 128:(q + 1) * 256, :] = d_up.T.astype(BF)

    upper, lower = pl.ds(0, hid), pl.ds(hid, hid)

    def z_of(k):
        return z_near[NZ - 1 - k]

    def product(k, halves=(0, 1)):
        zz = z_of(k)
        cols = recv[:, :, pl.ds(pl.multiple_of(zz * (NX * 128), 128), NX * 128)].reshape(
            NY * NC * CAP, NX * 128
        )
        for m in halves:
            got = dot(p_t[m * hid:(m + 1) * hid, :], cols).astype(BF)
            for xx in range(NX):
                g[zz, xx, m * hid:(m + 1) * hid, :] = got[:, xx * 128:(xx + 1) * 128]

    def sends(k):
        zz = z_of(k)
        return [
            remote(g.at[zz, across, upper], r_a.at[zz], rs_send.at[0, k], rs_recv.at[0, k], to_right),
            remote(g.at[zz, across, lower], r_b.at[zz], rs_send.at[1, k], rs_recv.at[1, k], to_left),
            remote(g.at[zz, right, lower], f_l.at[zz, lower], rs_send.at[2, k], rs_recv.at[2, k], to_right),
            remote(g.at[zz, left, upper], f_r.at[zz, upper], rs_send.at[3, k], rs_recv.at[3, k], to_left),
            remote(g.at[zz, right, upper], f_l.at[zz, upper], rs_send.at[4, k], rs_recv.at[4, k], to_right),
            remote(g.at[zz, left, lower], f_r.at[zz, lower], rs_send.at[5, k], rs_recv.at[5, k], to_left),
        ]

    rs = [sends(k) for k in range(NZ)]
    zs = [
        remote(
            g.at[z_of(k), x], z_buf.at[z], z_send.at[k], z_recv.at[z],
            {"blk": blk_of(x, z_of(k), c)},
        )
        for k in range(NZ - 1)
    ]

    def far_start(k):
        product(k)
        for cp in rs[k][:2]:
            cp.start()

    def near_start(k):
        for cp in rs[k][2:4]:
            cp.start()

    def pass_on(k):
        zz = z_of(k)
        rs[k][0].wait_recv()
        g[zz, right, upper] = (g[zz, right, upper].astype(F32) + r_a[zz].astype(F32)).astype(BF)
        rs[k][4].start()
        rs[k][1].wait_recv()
        g[zz, left, lower] = (g[zz, left, lower].astype(F32) + r_b[zz].astype(F32)).astype(BF)
        rs[k][5].start()

    def gathered(k):
        zz = z_of(k)
        for cp in rs[k][2:]:
            cp.wait_recv()
        return g[zz, x].astype(F32) + f_l[zz].astype(F32) + f_r[zz].astype(F32)

    def finish(k):
        g[z_of(k), x] = gathered(k).astype(BF)
        zs[k].start()

    swap_cot.wait_recv()
    backward(0)
    product(0, (0,))
    rs[0][0].start()
    rs[0][3].start()
    backward(1)
    product(0, (1,))
    rs[0][1].start()
    rs[0][2].start()
    far_start(1)
    near_start(1)
    far_start(2)
    pass_on(0)
    near_start(2)
    pass_on(1)
    product(3)
    pass_on(2)
    finish(0)
    for cp in rs[3][:4]:
        cp.start()
    finish(1)
    finish(2)
    pass_on(3)
    total = gathered(NZ - 1)
    for k in range(1, NZ):
        got = z_buf.at[z_near[k]]
        remote(got, got, z_send.at[k], z_recv.at[z_near[k]], partner).wait_recv()
        total = total + got[...].astype(F32)
    for q in range(hid // 128):
        for j in range(2):
            out_ref[:, j * hid + q * 128:j * hid + (q + 1) * 128] = (
                total[q * 256 + j * 128:q * 256 + (j + 1) * 128].T.astype(BF)
            )

    for cp in wz[1:] + direct + first_legs + second_legs + swaps + zs + [swap_cot, cross]:
        cp.wait_send()
    for group in wx + wr + rs:
        for cp in group:
            cp.wait_send()


def local(tokens, routed_experts, act_cotangent, weight_codes, weight_scales):
    rows, width = tokens.shape
    top, hid = act_cotangent.shape[1:]
    half = width // 2
    dma = pltpu.SemaphoreType.DMA
    hbm = pl.BlockSpec(memory_space=pltpu.HBM)
    out = pl.pallas_call(
        kernel,
        out_shape=jax.ShapeDtypeStruct((rows, 2 * hid), BF),
        in_specs=[hbm] * 5,
        out_specs=pl.BlockSpec(memory_space=pltpu.VMEM),
        scratch_shapes=[
            pltpu.VMEM((rows, width), BF),
            pltpu.VMEM((top, rows), jnp.int32),
            pltpu.VMEM((rows * top, hid), BF),
            pltpu.VMEM((rows, 1, 2, hid), BF),
            pltpu.VMEM((1, 1, 2, hid // 128), BF),
            pltpu.VMEM((rows, 2, hid), F32),
            pltpu.VMEM((rows, top, 128), F32),
            pltpu.VMEM((NY, NC, CAP, half + 128), BF),
            pltpu.VMEM((NY * NC, CAP, half + 128), BF),
            pltpu.VMEM((NC, CAP, half + 128), BF),
            pltpu.VMEM((NX * NZ, 128, 2 * hid), BF),
            pltpu.VMEM((2, NY * NC * CAP, hid), F32),
            pltpu.VMEM((2, NY * NC * CAP, hid), BF),
            pltpu.VMEM((2, NY * NC * CAP, hid), BF),
            pltpu.VMEM((NY * NC, CAP, 128), BF),
            pltpu.VMEM((2 * hid, NY * NC * CAP), BF),
            pltpu.VMEM((NZ, NX, 2 * hid, 128), BF),
            pltpu.VMEM((NZ, hid, 128), BF),
            pltpu.VMEM((NZ, hid, 128), BF),
            pltpu.VMEM((NZ, 2 * hid, 128), BF),
            pltpu.VMEM((NZ, 2 * hid, 128), BF),
            pltpu.VMEM((NZ, 2 * hid, 128), BF),
            dma((5,)), dma, pltpu.SemaphoreType.REGULAR,
            dma((16,)), dma((16,)), dma((2,)), dma((2,)),
            dma((NZ,)), dma((NZ,)), dma((4, NZ)), dma((4, NZ)),
            dma((3,)), dma((3,)),
            dma((6, NZ)), dma((6, NZ)), dma((NZ,)), dma((NZ,)),
        ],
        compiler_params=pltpu.CompilerParams(
            collective_id=0, has_side_effects=True, vmem_limit_bytes=48 * 1024 * 1024
        ),
    )(*[
        pltpu.with_memory_space_constraint(a, pltpu.HBM)
        for a in (
            tokens, routed_experts.T, act_cotangent.reshape(rows * top, hid),
            weight_codes, weight_scales,
        )
    ])
    return out.reshape(rows, 1, 2, hid)


def solution(mesh):
    return jax.shard_map(
        local,
        mesh=mesh,
        in_specs=(
            P(("group", "blk"), None),
            P(("group", "blk"), None),
            P(("group", "blk"), None, "att"),
            P("blk", "group", None, "att"),
            P("blk", "group", None, "att"),
        ),
        out_specs=P("blk", "group", None, "att"),
        check_vma=False,
    )
```

```python
import functools

import jax
import jax.numpy as jnp
from jax import lax
from jax.experimental import pallas as pl
from jax.experimental.pallas import tpu as pltpu
from jax.sharding import PartitionSpec as P

MESH = pl.DeviceIdType.MESH
CAP = 16
NY, NX, NZ, NC = 8, 4, 4, 2
BF = jnp.bfloat16
F32 = jnp.float32


def dot(a, b):
    return jnp.dot(a, b, preferred_element_type=F32)


def kernel(
    tokens_hbm, routed_hbm, act_hbm, codes_hbm, scales_hbm, out_ref,
    tok, routed, act, codes, scales, codes32, spread, send, recv, relay,
    w, part, part_sent, other, cot_other, p_t, g, r_a, r_b, f_l, f_r, z_buf,
    in_sem, own_sem, ready, a_send, a_recv, rl_send, rl_recv,
    wz_send, wz_recv, wx_send, wx_recv, ex_send, ex_recv,
    rs_send, rs_recv, z_send, z_recv,
):
    y = lax.axis_index("group")
    b = lax.axis_index("blk")
    x, z, c = b // (NZ * NC), (b // NC) % NZ, b % NC
    half = send.shape[3] - 128
    hid = act.shape[1]

    def blk_of(xx, zz, cc):
        return xx * (NZ * NC) + zz * NC + cc

    right, left, across = (x + 1) % NX, (x + NX - 1) % NX, (x + 2) % NX
    z_near = [z, z + 1 - 2 * (z % 2), 2 - z // 2, 3 - 3 * (z // 2)]
    to_right = {"blk": blk_of(right, z, c)}
    to_left = {"blk": blk_of(left, z, c)}
    partner = {"blk": blk_of(x, z, 1 - c)}

    def remote(src, dst, s_sem, r_sem, where):
        return pltpu.make_async_remote_copy(
            src_ref=src, dst_ref=dst, send_sem=s_sem, recv_sem=r_sem,
            device_id=where, device_id_type=MESH,
        )

    loads = [
        pltpu.make_async_copy(codes_hbm, codes, in_sem.at[0]),
        pltpu.make_async_copy(scales_hbm, scales, in_sem.at[1]),
        pltpu.make_async_copy(routed_hbm, routed, in_sem.at[2]),
        pltpu.make_async_copy(tokens_hbm, tok, in_sem.at[3]),
        pltpu.make_async_copy(act_hbm, act, in_sem.at[4]),
    ]
    for load in loads:
        load.start()

    peers = [(dy, x, z, cc) for dy in (1, 2, 3, 5, 6, 7) for cc in range(NC)]
    peers += [(0, x, z, 1 - c), (0, right, z, c), (0, left, z, c)]
    peers += [(0, x, (z + k) % NZ, c) for k in range(1, NZ)]

    def is_last(dy, xx, zz, cc):
        return ((y + dy) % NY == 0) & (blk_of(xx, zz, cc) == 0) & (lax.axis_index("att") == 0)

    def place(dy, xx, zz, cc):
        return {"group": (y + dy) % NY, "blk": blk_of(xx, zz, cc)}

    last = is_last(0, x, z, c)
    by_last = functools.reduce(lambda p, q: p | q, [is_last(*peer) for peer in peers])
    owed = by_last.astype(jnp.int32)
    barrier = pltpu.get_barrier_semaphore()

    @pl.when(jnp.logical_not(last))
    def _():
        for peer in peers:
            pl.semaphore_signal(barrier, inc=1, device_id=place(*peer), device_id_type=MESH)

    @pl.when(last)
    def _():
        pl.semaphore_wait(barrier, len(peers))
        for peer in peers:
            pl.semaphore_signal(ready, inc=1, device_id=place(*peer), device_id_type=MESH)

    loads[0].wait()
    loads[1].wait()
    codes32[...] = codes[:, 0].astype(F32)
    sc = scales[0, 0].astype(F32)
    mine_w = z * NX + x
    for j in range(2):
        for q in range(hid // 128):
            piece = codes32[:, j, q * 128:(q + 1) * 128] * sc[j:j + 1, q:q + 1]
            at = q * 256 + j * 128
            w[mine_w, :, at:at + 128] = piece.astype(BF)

    top, low = pl.ds(0, 64), pl.ds(64, 64)
    wz, wx, wr = [None], [], []
    for k in range(NZ):
        row_of = z_near[k] * NX
        here_w, left_w, right_w = w.at[row_of + x], w.at[row_of + left], w.at[row_of + right]
        if k:
            wz.append(remote(
                w.at[mine_w], w.at[mine_w], wz_send.at[k], wz_recv.at[z],
                {"blk": blk_of(x, z_near[k], c)},
            ))
        wx.append([
            remote(here_w, here_w, wx_send.at[0, k], wx_recv.at[0, k], to_right),
            remote(here_w, here_w, wx_send.at[1, k], wx_recv.at[1, k], to_left),
        ])
        wr.append([
            remote(left_w.at[top], left_w.at[top], wx_send.at[2, k], wx_recv.at[2, k], to_right),
            remote(right_w.at[low], right_w.at[low], wx_send.at[3, k], wx_recv.at[3, k], to_left),
        ])

    @pl.when(last)
    def _():
        for cp in wz[1:] + wx[0]:
            cp.start()

    loads[2].wait()
    ids = routed[...].T
    lane = lax.broadcasted_iota(jnp.int32, (128, 128), 1)
    row = lax.broadcasted_iota(jnp.int32, (128, 128), 0)
    expert_of, slot_of = lane // CAP, lane % CAP
    hits = [
        jnp.where(ids[:, k:k + 1] == expert_of, 1.0, 0.0) for k in range(ids.shape[1])
    ]
    chosen = functools.reduce(lambda p, q: p + q, hits)
    before = jnp.where(lane < row, 1.0, 0.0).astype(BF)
    position = dot(before, chosen.astype(BF))
    select = jnp.where(position == slot_of.astype(F32), chosen, 0.0)
    for k in range(len(hits)):
        spread[:, k, :] = select * hits[k]
    select_t = select.T.astype(BF)
    pick = spread[...].reshape(128 * len(hits), 128).astype(BF)
    loads[4].wait()
    cot = lax.dot_general(pick, act[...], (((0,), (0,)), ((), ())), preferred_element_type=F32)
    for j in range(NC):
        send[:, j, :, half:half + 128] = (
            cot[:, j * 128:(j + 1) * 128].astype(BF).reshape(NY, CAP, 128)
        )

    @pl.when(jnp.logical_not(last))
    def _():
        pl.semaphore_wait(barrier, len(peers) - owed)

    later_to, later_from, no = [], [], jnp.logical_not

    def do(waits, starts, to_last, from_last=None):
        def act():
            for cp in waits:
                cp.wait_recv()
            for cp in starts:
                cp.start()

        if from_last is None:
            pl.when(no(to_last))(act)
            later_to.append(([to_last], act))
        elif to_last is None:
            pl.when(no(from_last))(act)
            later_from.append(([from_last], act))
        else:
            pl.when(no(to_last) & no(from_last))(act)
            later_to.append(([to_last, no(from_last)], act))
            later_from.append(([from_last], act))

    right_last, left_last = is_last(0, right, z, c), is_last(0, left, z, c)

    near_last = [is_last(0, x, zz, c) for zz in z_near]

    @pl.when(jnp.logical_not(last))
    def _():
        for k in range(1, NZ):
            do([], [wz[k]], near_last[k])
        do([], [wx[0][0]], right_last)
        do([], [wx[0][1]], left_last)

    loads[3].wait()
    for pair in range(NX * NZ):
        rows = dot(select_t, tok[:, pair * 256:(pair + 1) * 256]).astype(BF)
        at = ((pair % NZ) * NX + pair // NZ) * 128
        for j in range(NC):
            send[:, j, :, at:at + 128] = rows[:, j * 128:(j + 1) * 128].reshape(NY, CAP, 128)

    here = y * NC + c
    first_legs, second_legs, direct = [], [], []
    for j in range(NC):
        dy = 2 if j == 0 else NY - 2
        cp = remote(
            send.at[(y + 4) % NY, j], relay.at[j], rl_send.at[j], rl_recv.at[j],
            {"group": (y + dy) % NY},
        )
        first_legs.append(cp)
        do([], [cp], is_last(dy, x, z, c))

    def rows_to(dy):
        to = (y + dy) % NY
        for j in range(NC):
            direct.append(remote(
                send.at[to, j], recv.at[here], a_send.at[len(direct)], a_recv.at[here],
                {"group": to, "blk": blk_of(x, z, j)},
            ))
        return direct[-NC:]

    for dy in (3, 5):
        for j, cp in enumerate(rows_to(dy)):
            do([], [cp], is_last(dy, x, z, j))
    own = pltpu.make_async_copy(send.at[y, c], recv.at[here], own_sem)
    own.start()

    def z_rows(k):
        near_w = w.at[z_near[k] * NX + x]
        return remote(near_w, near_w, wz_send.at[k], wz_recv.at[z_near[k]], partner)

    def pass_z(k):
        z_rows(k).wait_recv()
        for cp in wx[k]:
            cp.start()

    def pass_half(k):
        for cp, onward in zip(wx[k], wr[k]):
            cp.wait_recv()
            onward.start()

    do([z_rows(1)], [], None, near_last[1])
    do([], [wx[1][0]], right_last, near_last[1])
    do([], [wx[1][1]], left_last, near_last[1])

    @pl.when(by_last)
    def _():
        pl.semaphore_wait(ready, 1)
        for flags, act in later_to:
            pl.when(functools.reduce(lambda p, q: p & q, flags))(act)

    held = []
    for j in range(NC):
        back, on = (NY - 2, 2) if j == 0 else (2, NY - 2)
        slot = ((y + back) % NY) * NC + c
        second_legs.append(remote(
            relay.at[j], recv.at[slot], a_send.at[13 + j], a_recv.at[slot],
            {"group": (y + on) % NY, "blk": blk_of(x, z, j)},
        ))
        held.append(last | is_last(back, x, z, c))

    def pass_rows(j):
        first_legs[j].wait_recv()
        second_legs[j].start()

    for dy in (2, 6):
        for cp in rows_to(dy):
            cp.start()
    for j in range(NC):
        pl.when(no(held[j]))(functools.partial(pass_rows, j))
    for dy in (1, 7):
        for cp in rows_to(dy):
            cp.start()
    cross = remote(send.at[y, 1 - c], recv.at[here], a_send.at[12], a_recv.at[here], partner)
    cross.start()
    pass_z(2)
    pass_half(0)
    pass_z(3)

    @pl.when(by_last)
    def _():
        for flags, act in later_from:
            pl.when(functools.reduce(lambda p, q: p & q, flags))(act)

    pass_half(1)
    for j in range(NC):
        pl.when(held[j])(functools.partial(pass_rows, j))
    pass_half(2)
    pass_half(3)
    for k in range(NZ):
        for cp in wr[k]:
            cp.wait_recv()
    own.wait()
    for n in range(1, NY * NC):
        slot = (here + n) % (NY * NC)
        remote(
            recv.at[slot], recv.at[slot], a_send.at[15], a_recv.at[slot], partner
        ).wait_recv()

    swap_cot = remote(
        recv.at[:, :, pl.ds(half, 128)], cot_other, ex_send.at[2], ex_recv.at[2], partner
    )
    swap_cot.start()
    swaps = []
    rows_here = recv[:, :, :half].reshape(NY * NC * CAP, half)
    for q in range(hid // 128):
        part[q] = dot(rows_here, w[:, :, q * 256:(q + 1) * 256].reshape(half, 256))
        part_sent[q] = part[q].astype(BF)
        cp = remote(part_sent.at[q], other.at[q], ex_send.at[q], ex_recv.at[q], partner)
        cp.start()
        swaps.append(cp)

    def backward(q):
        swaps[q].wait_recv()
        gate = part[q, :, :128] + other[q, :, :128].astype(F32)
        up = part[q, :, 128:] + other[q, :, 128:].astype(F32)
        mine = recv[:, :, half:].reshape(NY * NC * CAP, 128).astype(F32)
        theirs = cot_other[...].reshape(NY * NC * CAP, 128).astype(F32)
        cotangent = jnp.where(c == q, mine, theirs)
        s = jax.nn.sigmoid(gate)
        d_gate = cotangent * up * s * (1.0 + gate * (1.0 - s))
        d_up = cotangent * gate * s
        p_t[q * 256:q * 256 + 128, :] = d_gate.T.astype(BF)
        p_t[q * 256 + 128:(q + 1) * 256, :] = d_up.T.astype(BF)

    upper, lower = pl.ds(0, hid), pl.ds(hid, hid)

    def z_of(k):
        return z_near[NZ - 1 - k]

    def product(k, halves=(0, 1)):
        zz = z_of(k)
        cols = recv[:, :, pl.ds(pl.multiple_of(zz * (NX * 128), 128), NX * 128)].reshape(
            NY * NC * CAP, NX * 128
        )
        for m in halves:
            got = dot(p_t[m * hid:(m + 1) * hid, :], cols).astype(BF)
            for xx in range(NX):
                g[zz, xx, m * hid:(m + 1) * hid, :] = got[:, xx * 128:(xx + 1) * 128]

    def sends(k):
        zz = z_of(k)
        return [
            remote(g.at[zz, across, upper], r_a.at[zz], rs_send.at[0, k], rs_recv.at[0, k], to_right),
            remote(g.at[zz, across, lower], r_b.at[zz], rs_send.at[1, k], rs_recv.at[1, k], to_left),
            remote(g.at[zz, right, lower], f_l.at[zz, lower], rs_send.at[2, k], rs_recv.at[2, k], to_right),
            remote(g.at[zz, left, upper], f_r.at[zz, upper], rs_send.at[3, k], rs_recv.at[3, k], to_left),
            remote(g.at[zz, right, upper], f_l.at[zz, upper], rs_send.at[4, k], rs_recv.at[4, k], to_right),
            remote(g.at[zz, left, lower], f_r.at[zz, lower], rs_send.at[5, k], rs_recv.at[5, k], to_left),
        ]

    rs = [sends(k) for k in range(NZ)]
    zs = [
        remote(
            g.at[z_of(k), x], z_buf.at[z], z_send.at[k], z_recv.at[z],
            {"blk": blk_of(x, z_of(k), c)},
        )
        for k in range(NZ - 1)
    ]

    def far_start(k):
        product(k)
        for cp in rs[k][:2]:
            cp.start()

    def near_start(k):
        for cp in rs[k][2:4]:
            cp.start()

    def pass_on(k):
        zz = z_of(k)
        rs[k][0].wait_recv()
        g[zz, right, upper] = (g[zz, right, upper].astype(F32) + r_a[zz].astype(F32)).astype(BF)
        rs[k][4].start()
        rs[k][1].wait_recv()
        g[zz, left, lower] = (g[zz, left, lower].astype(F32) + r_b[zz].astype(F32)).astype(BF)
        rs[k][5].start()

    def gathered(k):
        zz = z_of(k)
        for cp in rs[k][2:]:
            cp.wait_recv()
        return g[zz, x].astype(F32) + f_l[zz].astype(F32) + f_r[zz].astype(F32)

    def finish(k):
        g[z_of(k), x] = gathered(k).astype(BF)
        zs[k].start()

    swap_cot.wait_recv()
    backward(0)
    product(0, (0,))
    rs[0][0].start()
    rs[0][3].start()
    backward(1)
    product(0, (1,))
    rs[0][1].start()
    rs[0][2].start()
    far_start(1)
    pass_on(0)
    near_start(1)
    far_start(2)
    pass_on(1)
    finish(0)
    near_start(2)
    far_start(3)
    pass_on(2)
    near_start(3)
    finish(1)
    pass_on(3)
    finish(2)
    total = gathered(NZ - 1)
    for k in range(1, NZ):
        got = z_buf.at[z_near[k]]
        remote(got, got, z_send.at[k], z_recv.at[z_near[k]], partner).wait_recv()
        total = total + got[...].astype(F32)
    for q in range(hid // 128):
        for j in range(2):
            out_ref[:, j * hid + q * 128:j * hid + (q + 1) * 128] = (
                total[q * 256 + j * 128:q * 256 + (j + 1) * 128].T.astype(BF)
            )

    for cp in wz[1:] + direct + first_legs + second_legs + swaps + zs + [swap_cot, cross]:
        cp.wait_send()
    for group in wx + wr + rs:
        for cp in group:
            cp.wait_send()


def local(tokens, routed_experts, act_cotangent, weight_codes, weight_scales):
    rows, width = tokens.shape
    top, hid = act_cotangent.shape[1:]
    half = width // 2
    dma = pltpu.SemaphoreType.DMA
    hbm = pl.BlockSpec(memory_space=pltpu.HBM)
    out = pl.pallas_call(
        kernel,
        out_shape=jax.ShapeDtypeStruct((rows, 2 * hid), BF),
        in_specs=[hbm] * 5,
        out_specs=pl.BlockSpec(memory_space=pltpu.VMEM),
        scratch_shapes=[
            pltpu.VMEM((rows, width), BF),
            pltpu.VMEM((top, rows), jnp.int32),
            pltpu.VMEM((rows * top, hid), BF),
            pltpu.VMEM((rows, 1, 2, hid), BF),
            pltpu.VMEM((1, 1, 2, hid // 128), BF),
            pltpu.VMEM((rows, 2, hid), F32),
            pltpu.VMEM((rows, top, 128), F32),
            pltpu.VMEM((NY, NC, CAP, half + 128), BF),
            pltpu.VMEM((NY * NC, CAP, half + 128), BF),
            pltpu.VMEM((NC, CAP, half + 128), BF),
            pltpu.VMEM((NX * NZ, 128, 2 * hid), BF),
            pltpu.VMEM((2, NY * NC * CAP, hid), F32),
            pltpu.VMEM((2, NY * NC * CAP, hid), BF),
            pltpu.VMEM((2, NY * NC * CAP, hid), BF),
            pltpu.VMEM((NY * NC, CAP, 128), BF),
            pltpu.VMEM((2 * hid, NY * NC * CAP), BF),
            pltpu.VMEM((NZ, NX, 2 * hid, 128), BF),
            pltpu.VMEM((NZ, hid, 128), BF),
            pltpu.VMEM((NZ, hid, 128), BF),
            pltpu.VMEM((NZ, 2 * hid, 128), BF),
            pltpu.VMEM((NZ, 2 * hid, 128), BF),
            pltpu.VMEM((NZ, 2 * hid, 128), BF),
            dma((5,)), dma, pltpu.SemaphoreType.REGULAR,
            dma((16,)), dma((16,)), dma((2,)), dma((2,)),
            dma((NZ,)), dma((NZ,)), dma((4, NZ)), dma((4, NZ)),
            dma((3,)), dma((3,)),
            dma((6, NZ)), dma((6, NZ)), dma((NZ,)), dma((NZ,)),
        ],
        compiler_params=pltpu.CompilerParams(
            collective_id=0, has_side_effects=True, vmem_limit_bytes=48 * 1024 * 1024
        ),
    )(*[
        pltpu.with_memory_space_constraint(a, pltpu.HBM)
        for a in (
            tokens, routed_experts.T, act_cotangent.reshape(rows * top, hid),
            weight_codes, weight_scales,
        )
    ])
    return out.reshape(rows, 1, 2, hid)


def solution(mesh):
    return jax.shard_map(
        local,
        mesh=mesh,
        in_specs=(
            P(("group", "blk"), None),
            P(("group", "blk"), None),
            P(("group", "blk"), None, "att"),
            P("blk", "group", None, "att"),
            P("blk", "group", None, "att"),
        ),
        out_specs=P("blk", "group", None, "att"),
        check_vma=False,
    )
```

```python
import functools

import jax
import jax.numpy as jnp
from jax import lax
from jax.experimental import pallas as pl
from jax.experimental.pallas import tpu as pltpu
from jax.sharding import PartitionSpec as P

MESH = pl.DeviceIdType.MESH
CAP = 16
NY, NX, NZ, NC = 8, 4, 4, 2
BF = jnp.bfloat16
F32 = jnp.float32


def dot(a, b):
    return jnp.dot(a, b, preferred_element_type=F32)


def kernel(
    tokens_hbm, routed_hbm, act_hbm, codes_hbm, scales_hbm, out_ref,
    tok, routed, act, codes, scales, codes32, spread, send, recv, relay,
    w, part, part_sent, other, cot_other, p_t, g, r_a, r_b, f_l, f_r, z_buf,
    in_sem, own_sem, ready, a_send, a_recv, rl_send, rl_recv,
    wz_send, wz_recv, wx_send, wx_recv, ex_send, ex_recv,
    rs_send, rs_recv, z_send, z_recv,
):
    y = lax.axis_index("group")
    b = lax.axis_index("blk")
    x, z, c = b // (NZ * NC), (b // NC) % NZ, b % NC
    half = send.shape[3] - 128
    hid = act.shape[1]

    def blk_of(xx, zz, cc):
        return xx * (NZ * NC) + zz * NC + cc

    right, left, across = (x + 1) % NX, (x + NX - 1) % NX, (x + 2) % NX
    z_near = [z, z + 1 - 2 * (z % 2), 2 - z // 2, 3 - 3 * (z // 2)]
    to_right = {"blk": blk_of(right, z, c)}
    to_left = {"blk": blk_of(left, z, c)}
    partner = {"blk": blk_of(x, z, 1 - c)}

    def remote(src, dst, s_sem, r_sem, where):
        return pltpu.make_async_remote_copy(
            src_ref=src, dst_ref=dst, send_sem=s_sem, recv_sem=r_sem,
            device_id=where, device_id_type=MESH,
        )

    loads = [
        pltpu.make_async_copy(codes_hbm, codes, in_sem.at[0]),
        pltpu.make_async_copy(scales_hbm, scales, in_sem.at[1]),
        pltpu.make_async_copy(routed_hbm, routed, in_sem.at[2]),
        pltpu.make_async_copy(tokens_hbm, tok, in_sem.at[3]),
        pltpu.make_async_copy(act_hbm, act, in_sem.at[4]),
    ]
    for load in loads:
        load.start()

    peers = [(dy, x, z, cc) for dy in (1, 2, 3, 5, 6, 7) for cc in range(NC)]
    peers += [(0, x, z, 1 - c), (0, right, z, c), (0, left, z, c)]
    peers += [(0, x, (z + k) % NZ, c) for k in range(1, NZ)]

    def is_last(dy, xx, zz, cc):
        return ((y + dy) % NY == 0) & (blk_of(xx, zz, cc) == 0) & (lax.axis_index("att") == 0)

    def place(dy, xx, zz, cc):
        return {"group": (y + dy) % NY, "blk": blk_of(xx, zz, cc)}

    last = is_last(0, x, z, c)
    by_last = functools.reduce(lambda p, q: p | q, [is_last(*peer) for peer in peers])
    owed = by_last.astype(jnp.int32)
    barrier = pltpu.get_barrier_semaphore()

    @pl.when(jnp.logical_not(last))
    def _():
        for peer in peers:
            pl.semaphore_signal(barrier, inc=1, device_id=place(*peer), device_id_type=MESH)

    @pl.when(last)
    def _():
        pl.semaphore_wait(barrier, len(peers))
        for peer in peers:
            pl.semaphore_signal(ready, inc=1, device_id=place(*peer), device_id_type=MESH)

    loads[0].wait()
    loads[1].wait()
    codes32[...] = codes[:, 0].astype(F32)
    sc = scales[0, 0].astype(F32)
    mine_w = z * NX + x
    for j in range(2):
        for q in range(hid // 128):
            piece = codes32[:, j, q * 128:(q + 1) * 128] * sc[j:j + 1, q:q + 1]
            at = q * 256 + j * 128
            w[mine_w, :, at:at + 128] = piece.astype(BF)

    top, low = pl.ds(0, 64), pl.ds(64, 64)
    wz, wx, wr = [None], [], []
    for k in range(NZ):
        row_of = z_near[k] * NX
        here_w, left_w, right_w = w.at[row_of + x], w.at[row_of + left], w.at[row_of + right]
        if k:
            wz.append(remote(
                w.at[mine_w], w.at[mine_w], wz_send.at[k], wz_recv.at[z],
                {"blk": blk_of(x, z_near[k], c)},
            ))
        wx.append([
            remote(here_w, here_w, wx_send.at[0, k], wx_recv.at[0, k], to_right),
            remote(here_w, here_w, wx_send.at[1, k], wx_recv.at[1, k], to_left),
        ])
        wr.append([
            remote(left_w.at[top], left_w.at[top], wx_send.at[2, k], wx_recv.at[2, k], to_right),
            remote(right_w.at[low], right_w.at[low], wx_send.at[3, k], wx_recv.at[3, k], to_left),
        ])

    @pl.when(last)
    def _():
        for cp in wz[1:] + wx[0]:
            cp.start()

    loads[2].wait()
    ids = routed[...].T
    lane = lax.broadcasted_iota(jnp.int32, (128, 128), 1)
    row = lax.broadcasted_iota(jnp.int32, (128, 128), 0)
    expert_of, slot_of = lane // CAP, lane % CAP
    hits = [
        jnp.where(ids[:, k:k + 1] == expert_of, 1.0, 0.0) for k in range(ids.shape[1])
    ]
    chosen = functools.reduce(lambda p, q: p + q, hits)
    before = jnp.where(lane < row, 1.0, 0.0).astype(BF)
    position = dot(before, chosen.astype(BF))
    select = jnp.where(position == slot_of.astype(F32), chosen, 0.0)
    for k in range(len(hits)):
        spread[:, k, :] = select * hits[k]
    select_t = select.T.astype(BF)
    pick = spread[...].reshape(128 * len(hits), 128).astype(BF)
    loads[4].wait()
    cot = lax.dot_general(pick, act[...], (((0,), (0,)), ((), ())), preferred_element_type=F32)
    for j in range(NC):
        send[:, j, :, half:half + 128] = (
            cot[:, j * 128:(j + 1) * 128].astype(BF).reshape(NY, CAP, 128)
        )

    @pl.when(jnp.logical_not(last))
    def _():
        pl.semaphore_wait(barrier, len(peers) - owed)

    later_to, later_from, no = [], [], jnp.logical_not

    def do(waits, starts, to_last, from_last=None):
        def act():
            for cp in waits:
                cp.wait_recv()
            for cp in starts:
                cp.start()

        if from_last is None:
            pl.when(no(to_last))(act)
            later_to.append(([to_last], act))
        elif to_last is None:
            pl.when(no(from_last))(act)
            later_from.append(([from_last], act))
        else:
            pl.when(no(to_last) & no(from_last))(act)
            later_to.append(([to_last, no(from_last)], act))
            later_from.append(([from_last], act))

    right_last, left_last = is_last(0, right, z, c), is_last(0, left, z, c)

    near_last = [is_last(0, x, zz, c) for zz in z_near]

    @pl.when(jnp.logical_not(last))
    def _():
        for k in range(1, NZ):
            do([], [wz[k]], near_last[k])
        do([], [wx[0][0]], right_last)
        do([], [wx[0][1]], left_last)

    loads[3].wait()
    for pair in range(NX * NZ):
        rows = dot(select_t, tok[:, pair * 256:(pair + 1) * 256]).astype(BF)
        at = ((pair % NZ) * NX + pair // NZ) * 128
        for j in range(NC):
            send[:, j, :, at:at + 128] = rows[:, j * 128:(j + 1) * 128].reshape(NY, CAP, 128)

    here = y * NC + c
    first_legs, second_legs, direct = [], [], []
    for j in range(NC):
        dy = 2 if j == 0 else NY - 2
        cp = remote(
            send.at[(y + 4) % NY, j], relay.at[j], rl_send.at[j], rl_recv.at[j],
            {"group": (y + dy) % NY},
        )
        first_legs.append(cp)
        do([], [cp], is_last(dy, x, z, c))

    def rows_to(dy):
        to = (y + dy) % NY
        for j in range(NC):
            direct.append(remote(
                send.at[to, j], recv.at[here], a_send.at[len(direct)], a_recv.at[here],
                {"group": to, "blk": blk_of(x, z, j)},
            ))
        return direct[-NC:]

    for dy in (3, 5):
        for j, cp in enumerate(rows_to(dy)):
            do([], [cp], is_last(dy, x, z, j))
    own = pltpu.make_async_copy(send.at[y, c], recv.at[here], own_sem)
    own.start()

    def z_rows(k):
        near_w = w.at[z_near[k] * NX + x]
        return remote(near_w, near_w, wz_send.at[k], wz_recv.at[z_near[k]], partner)

    def pass_z(k):
        z_rows(k).wait_recv()
        for cp in wx[k]:
            cp.start()

    def pass_half(k):
        for cp, onward in zip(wx[k], wr[k]):
            cp.wait_recv()
            onward.start()

    rest = []
    for dy in (2, 6, 1, 7):
        for j, cp in enumerate(rows_to(dy)):
            flag = is_last(dy, x, z, j)
            later_to.append(([flag], cp.start))
            rest.append((pl.when(no(flag)), cp))

    do([z_rows(1)], [], None, near_last[1])
    do([], [wx[1][0]], right_last, near_last[1])
    do([], [wx[1][1]], left_last, near_last[1])

    @pl.when(by_last)
    def _():
        pl.semaphore_wait(ready, 1)
        for flags, act in later_to:
            pl.when(functools.reduce(lambda p, q: p & q, flags))(act)

    held = []
    for j in range(NC):
        back, on = (NY - 2, 2) if j == 0 else (2, NY - 2)
        slot = ((y + back) % NY) * NC + c
        second_legs.append(remote(
            relay.at[j], recv.at[slot], a_send.at[13 + j], a_recv.at[slot],
            {"group": (y + on) % NY, "blk": blk_of(x, z, j)},
        ))
        held.append(last | is_last(back, x, z, c))

    def pass_rows(j):
        first_legs[j].wait_recv()
        second_legs[j].start()

    for unless_last, cp in rest[:4]:
        unless_last(cp.start)
    for j in range(NC):
        pl.when(no(held[j]))(functools.partial(pass_rows, j))
    for unless_last, cp in rest[4:]:
        unless_last(cp.start)
    cross = remote(send.at[y, 1 - c], recv.at[here], a_send.at[12], a_recv.at[here], partner)
    cross.start()
    pass_z(2)
    pass_half(0)
    pass_z(3)

    @pl.when(by_last)
    def _():
        for flags, act in later_from:
            pl.when(functools.reduce(lambda p, q: p & q, flags))(act)

    pass_half(1)
    for j in range(NC):
        pl.when(held[j])(functools.partial(pass_rows, j))
    pass_half(2)
    pass_half(3)
    for k in range(NZ):
        for cp in wr[k]:
            cp.wait_recv()
    own.wait()
    for n in range(1, NY * NC):
        slot = (here + n) % (NY * NC)
        remote(
            recv.at[slot], recv.at[slot], a_send.at[15], a_recv.at[slot], partner
        ).wait_recv()

    swap_cot = remote(
        recv.at[:, :, pl.ds(half, 128)], cot_other, ex_send.at[2], ex_recv.at[2], partner
    )
    swap_cot.start()
    swaps = []
    rows_here = recv[:, :, :half].reshape(NY * NC * CAP, half)
    for q in range(hid // 128):
        part[q] = dot(rows_here, w[:, :, q * 256:(q + 1) * 256].reshape(half, 256))
        part_sent[q] = part[q].astype(BF)
        cp = remote(part_sent.at[q], other.at[q], ex_send.at[q], ex_recv.at[q], partner)
        cp.start()
        swaps.append(cp)

    def backward(q):
        swaps[q].wait_recv()
        gate = part[q, :, :128] + other[q, :, :128].astype(F32)
        up = part[q, :, 128:] + other[q, :, 128:].astype(F32)
        mine = recv[:, :, half:].reshape(NY * NC * CAP, 128).astype(F32)
        theirs = cot_other[...].reshape(NY * NC * CAP, 128).astype(F32)
        cotangent = jnp.where(c == q, mine, theirs)
        s = jax.nn.sigmoid(gate)
        d_gate = cotangent * up * s * (1.0 + gate * (1.0 - s))
        d_up = cotangent * gate * s
        p_t[q * 256:q * 256 + 128, :] = d_gate.T.astype(BF)
        p_t[q * 256 + 128:(q + 1) * 256, :] = d_up.T.astype(BF)

    upper, lower = pl.ds(0, hid), pl.ds(hid, hid)

    def z_of(k):
        return z_near[NZ - 1 - k]

    def product(k, halves=(0, 1)):
        zz = z_of(k)
        cols = recv[:, :, pl.ds(pl.multiple_of(zz * (NX * 128), 128), NX * 128)].reshape(
            NY * NC * CAP, NX * 128
        )
        for m in halves:
            got = dot(p_t[m * hid:(m + 1) * hid, :], cols).astype(BF)
            for xx in range(NX):
                g[zz, xx, m * hid:(m + 1) * hid, :] = got[:, xx * 128:(xx + 1) * 128]

    def sends(k):
        zz = z_of(k)
        return [
            remote(g.at[zz, across, upper], r_a.at[zz], rs_send.at[0, k], rs_recv.at[0, k], to_right),
            remote(g.at[zz, across, lower], r_b.at[zz], rs_send.at[1, k], rs_recv.at[1, k], to_left),
            remote(g.at[zz, right, lower], f_l.at[zz, lower], rs_send.at[2, k], rs_recv.at[2, k], to_right),
            remote(g.at[zz, left, upper], f_r.at[zz, upper], rs_send.at[3, k], rs_recv.at[3, k], to_left),
            remote(g.at[zz, right, upper], f_l.at[zz, upper], rs_send.at[4, k], rs_recv.at[4, k], to_right),
            remote(g.at[zz, left, lower], f_r.at[zz, lower], rs_send.at[5, k], rs_recv.at[5, k], to_left),
        ]

    rs = [sends(k) for k in range(NZ)]
    zs = [
        remote(
            g.at[z_of(k), x], z_buf.at[z], z_send.at[k], z_recv.at[z],
            {"blk": blk_of(x, z_of(k), c)},
        )
        for k in range(NZ - 1)
    ]

    def far_start(k):
        product(k)
        for cp in rs[k][:2]:
            cp.start()

    def near_start(k):
        for cp in rs[k][2:4]:
            cp.start()

    def pass_on(k):
        zz = z_of(k)
        rs[k][0].wait_recv()
        g[zz, right, upper] = (g[zz, right, upper].astype(F32) + r_a[zz].astype(F32)).astype(BF)
        rs[k][4].start()
        rs[k][1].wait_recv()
        g[zz, left, lower] = (g[zz, left, lower].astype(F32) + r_b[zz].astype(F32)).astype(BF)
        rs[k][5].start()

    def gathered(k):
        zz = z_of(k)
        for cp in rs[k][2:]:
            cp.wait_recv()
        return g[zz, x].astype(F32) + f_l[zz].astype(F32) + f_r[zz].astype(F32)

    def finish(k):
        g[z_of(k), x] = gathered(k).astype(BF)
        zs[k].start()

    swap_cot.wait_recv()
    backward(0)
    product(0, (0,))
    rs[0][0].start()
    rs[0][3].start()
    backward(1)
    product(0, (1,))
    rs[0][1].start()
    rs[0][2].start()
    far_start(1)
    pass_on(0)
    near_start(1)
    far_start(2)
    pass_on(1)
    finish(0)
    near_start(2)
    far_start(3)
    pass_on(2)
    near_start(3)
    finish(1)
    pass_on(3)
    finish(2)
    def from_z(k):
        got = z_buf.at[z_near[k]]
        remote(got, got, z_send.at[k], z_recv.at[z_near[k]], partner).wait_recv()
        return got[...].astype(F32)

    total = from_z(3) + gathered(NZ - 1)
    total = total + from_z(2) + from_z(1)
    for q in range(hid // 128):
        for j in range(2):
            out_ref[:, j * hid + q * 128:j * hid + (q + 1) * 128] = (
                total[q * 256 + j * 128:q * 256 + (j + 1) * 128].T.astype(BF)
            )

    for cp in wz[1:] + direct + first_legs + second_legs + swaps + zs + [swap_cot, cross]:
        cp.wait_send()
    for group in wx + wr + rs:
        for cp in group:
            cp.wait_send()


def local(tokens, routed_experts, act_cotangent, weight_codes, weight_scales):
    rows, width = tokens.shape
    top, hid = act_cotangent.shape[1:]
    half = width // 2
    dma = pltpu.SemaphoreType.DMA
    hbm = pl.BlockSpec(memory_space=pltpu.HBM)
    out = pl.pallas_call(
        kernel,
        out_shape=jax.ShapeDtypeStruct((rows, 2 * hid), BF),
        in_specs=[hbm] * 5,
        out_specs=pl.BlockSpec(memory_space=pltpu.VMEM),
        scratch_shapes=[
            pltpu.VMEM((rows, width), BF),
            pltpu.VMEM((top, rows), jnp.int32),
            pltpu.VMEM((rows * top, hid), BF),
            pltpu.VMEM((rows, 1, 2, hid), BF),
            pltpu.VMEM((1, 1, 2, hid // 128), BF),
            pltpu.VMEM((rows, 2, hid), F32),
            pltpu.VMEM((rows, top, 128), F32),
            pltpu.VMEM((NY, NC, CAP, half + 128), BF),
            pltpu.VMEM((NY * NC, CAP, half + 128), BF),
            pltpu.VMEM((NC, CAP, half + 128), BF),
            pltpu.VMEM((NX * NZ, 128, 2 * hid), BF),
            pltpu.VMEM((2, NY * NC * CAP, hid), F32),
            pltpu.VMEM((2, NY * NC * CAP, hid), BF),
            pltpu.VMEM((2, NY * NC * CAP, hid), BF),
            pltpu.VMEM((NY * NC, CAP, 128), BF),
            pltpu.VMEM((2 * hid, NY * NC * CAP), BF),
            pltpu.VMEM((NZ, NX, 2 * hid, 128), BF),
            pltpu.VMEM((NZ, hid, 128), BF),
            pltpu.VMEM((NZ, hid, 128), BF),
            pltpu.VMEM((NZ, 2 * hid, 128), BF),
            pltpu.VMEM((NZ, 2 * hid, 128), BF),
            pltpu.VMEM((NZ, 2 * hid, 128), BF),
            dma((5,)), dma, pltpu.SemaphoreType.REGULAR,
            dma((16,)), dma((16,)), dma((2,)), dma((2,)),
            dma((NZ,)), dma((NZ,)), dma((4, NZ)), dma((4, NZ)),
            dma((3,)), dma((3,)),
            dma((6, NZ)), dma((6, NZ)), dma((NZ,)), dma((NZ,)),
        ],
        compiler_params=pltpu.CompilerParams(
            collective_id=0, has_side_effects=True, vmem_limit_bytes=48 * 1024 * 1024
        ),
    )(*[
        pltpu.with_memory_space_constraint(a, pltpu.HBM)
        for a in (
            tokens, routed_experts.T, act_cotangent.reshape(rows * top, hid),
            weight_codes, weight_scales,
        )
    ])
    return out.reshape(rows, 1, 2, hid)


def solution(mesh):
    return jax.shard_map(
        local,
        mesh=mesh,
        in_specs=(
            P(("group", "blk"), None),
            P(("group", "blk"), None),
            P(("group", "blk"), None, "att"),
            P("blk", "group", None, "att"),
            P("blk", "group", None, "att"),
        ),
        out_specs=P("blk", "group", None, "att"),
        check_vma=False,
    )
```

```python
import functools

import jax
import jax.numpy as jnp
from jax import lax
from jax.experimental import pallas as pl
from jax.experimental.pallas import tpu as pltpu
from jax.sharding import PartitionSpec as P

MESH = pl.DeviceIdType.MESH
CAP = 16
NY, NX, NZ, NC = 8, 4, 4, 2
BF = jnp.bfloat16
F32 = jnp.float32


def dot(a, b):
    return jnp.dot(a, b, preferred_element_type=F32)


def kernel(
    tokens_hbm, routed_hbm, act_hbm, codes_hbm, scales_hbm, out_ref,
    tok, routed, act, codes, scales, codes32, spread, send, recv, relay,
    w, part, part_sent, other, cot_other, p_t, g, r_a, r_b, f_l, f_r, z_buf,
    in_sem, own_sem, ready, a_send, a_recv, rl_send, rl_recv,
    wz_send, wz_recv, wx_send, wx_recv, ex_send, ex_recv,
    rs_send, rs_recv, z_send, z_recv,
):
    y = lax.axis_index("group")
    b = lax.axis_index("blk")
    x, z, c = b // (NZ * NC), (b // NC) % NZ, b % NC
    half = send.shape[3] - 128
    hid = act.shape[1]

    def blk_of(xx, zz, cc):
        return xx * (NZ * NC) + zz * NC + cc

    right, left, across = (x + 1) % NX, (x + NX - 1) % NX, (x + 2) % NX
    z_near = [z, z + 1 - 2 * (z % 2), 2 - z // 2, 3 - 3 * (z // 2)]
    to_right = {"blk": blk_of(right, z, c)}
    to_left = {"blk": blk_of(left, z, c)}
    partner = {"blk": blk_of(x, z, 1 - c)}

    def remote(src, dst, s_sem, r_sem, where):
        return pltpu.make_async_remote_copy(
            src_ref=src, dst_ref=dst, send_sem=s_sem, recv_sem=r_sem,
            device_id=where, device_id_type=MESH,
        )

    loads = [
        pltpu.make_async_copy(codes_hbm, codes, in_sem.at[0]),
        pltpu.make_async_copy(scales_hbm, scales, in_sem.at[1]),
        pltpu.make_async_copy(routed_hbm, routed, in_sem.at[2]),
        pltpu.make_async_copy(tokens_hbm, tok, in_sem.at[3]),
        pltpu.make_async_copy(act_hbm, act, in_sem.at[4]),
    ]
    for load in loads:
        load.start()

    peers = [(dy, x, z, cc) for dy in (1, 2, 3, 5, 6, 7) for cc in range(NC)]
    peers += [(0, x, z, 1 - c), (0, right, z, c), (0, left, z, c)]
    peers += [(0, x, (z + k) % NZ, c) for k in range(1, NZ)]

    def is_last(dy, xx, zz, cc):
        return ((y + dy) % NY == 0) & (blk_of(xx, zz, cc) == 0) & (lax.axis_index("att") == 0)

    def place(dy, xx, zz, cc):
        return {"group": (y + dy) % NY, "blk": blk_of(xx, zz, cc)}

    last = is_last(0, x, z, c)
    by_last = functools.reduce(lambda p, q: p | q, [is_last(*peer) for peer in peers])
    owed = by_last.astype(jnp.int32)
    barrier = pltpu.get_barrier_semaphore()

    @pl.when(jnp.logical_not(last))
    def _():
        for peer in peers:
            pl.semaphore_signal(barrier, inc=1, device_id=place(*peer), device_id_type=MESH)

    @pl.when(last)
    def _():
        pl.semaphore_wait(barrier, len(peers))
        for peer in peers:
            pl.semaphore_signal(ready, inc=1, device_id=place(*peer), device_id_type=MESH)

    loads[0].wait()
    loads[1].wait()
    codes32[...] = codes[:, 0].astype(F32)
    sc = scales[0, 0].astype(F32)
    mine_w = z * NX + x
    for j in range(2):
        for q in range(hid // 128):
            piece = codes32[:, j, q * 128:(q + 1) * 128] * sc[j:j + 1, q:q + 1]
            at = q * 256 + j * 128
            w[mine_w, :, at:at + 128] = piece.astype(BF)

    top, low = pl.ds(0, 64), pl.ds(64, 64)
    wz, wx, wr = [None], [], []
    for k in range(NZ):
        row_of = z_near[k] * NX
        here_w, left_w, right_w = w.at[row_of + x], w.at[row_of + left], w.at[row_of + right]
        if k:
            wz.append(remote(
                w.at[mine_w], w.at[mine_w], wz_send.at[k], wz_recv.at[z],
                {"blk": blk_of(x, z_near[k], c)},
            ))
        wx.append([
            remote(here_w, here_w, wx_send.at[0, k], wx_recv.at[0, k], to_right),
            remote(here_w, here_w, wx_send.at[1, k], wx_recv.at[1, k], to_left),
        ])
        wr.append([
            remote(left_w.at[top], left_w.at[top], wx_send.at[2, k], wx_recv.at[2, k], to_right),
            remote(right_w.at[low], right_w.at[low], wx_send.at[3, k], wx_recv.at[3, k], to_left),
        ])

    @pl.when(last)
    def _():
        for cp in wz[1:] + wx[0]:
            cp.start()

    loads[2].wait()
    ids = routed[...].T
    lane = lax.broadcasted_iota(jnp.int32, (128, 128), 1)
    row = lax.broadcasted_iota(jnp.int32, (128, 128), 0)
    expert_of, slot_of = lane // CAP, lane % CAP
    hits = [
        jnp.where(ids[:, k:k + 1] == expert_of, 1.0, 0.0) for k in range(ids.shape[1])
    ]
    chosen = functools.reduce(lambda p, q: p + q, hits)
    before = jnp.where(lane < row, 1.0, 0.0).astype(BF)
    position = dot(before, chosen.astype(BF))
    select = jnp.where(position == slot_of.astype(F32), chosen, 0.0)
    for k in range(len(hits)):
        spread[:, k, :] = select * hits[k]
    select_t = select.T.astype(BF)
    pick = spread[...].reshape(128 * len(hits), 128).astype(BF)
    loads[4].wait()
    cot = lax.dot_general(pick, act[...], (((0,), (0,)), ((), ())), preferred_element_type=F32)
    for j in range(NC):
        send[:, j, :, half:half + 128] = (
            cot[:, j * 128:(j + 1) * 128].astype(BF).reshape(NY, CAP, 128)
        )

    @pl.when(jnp.logical_not(last))
    def _():
        pl.semaphore_wait(barrier, len(peers) - owed)

    later_to, later_from, no = [], [], jnp.logical_not

    def do(waits, starts, to_last, from_last=None):
        def act():
            for cp in waits:
                cp.wait_recv()
            for cp in starts:
                cp.start()

        if from_last is None:
            pl.when(no(to_last))(act)
            later_to.append(([to_last], act))
        elif to_last is None:
            pl.when(no(from_last))(act)
            later_from.append(([from_last], act))
        else:
            pl.when(no(to_last) & no(from_last))(act)
            later_to.append(([to_last, no(from_last)], act))
            later_from.append(([from_last], act))

    right_last, left_last = is_last(0, right, z, c), is_last(0, left, z, c)

    near_last = [is_last(0, x, zz, c) for zz in z_near]

    @pl.when(jnp.logical_not(last))
    def _():
        for k in range(1, NZ):
            do([], [wz[k]], near_last[k])
        do([], [wx[0][0]], right_last)
        do([], [wx[0][1]], left_last)

    loads[3].wait()
    for pair in range(NX * NZ):
        rows = dot(select_t, tok[:, pair * 256:(pair + 1) * 256]).astype(BF)
        at = ((pair % NZ) * NX + pair // NZ) * 128
        for j in range(NC):
            send[:, j, :, at:at + 128] = rows[:, j * 128:(j + 1) * 128].reshape(NY, CAP, 128)

    here = y * NC + c
    first_legs, second_legs, direct = [], [], []
    for j in range(NC):
        dy = 2 if j == 0 else NY - 2
        cp = remote(
            send.at[(y + 4) % NY, j], relay.at[j], rl_send.at[j], rl_recv.at[j],
            {"group": (y + dy) % NY},
        )
        first_legs.append(cp)
        do([], [cp], is_last(dy, x, z, c))

    def rows_to(dy):
        to = (y + dy) % NY
        for j in range(NC):
            direct.append(remote(
                send.at[to, j], recv.at[here], a_send.at[len(direct)], a_recv.at[here],
                {"group": to, "blk": blk_of(x, z, j)},
            ))
        return direct[-NC:]

    for dy in (3, 5):
        for j, cp in enumerate(rows_to(dy)):
            do([], [cp], is_last(dy, x, z, j))
    own = pltpu.make_async_copy(send.at[y, c], recv.at[here], own_sem)
    own.start()

    def z_rows(k):
        near_w = w.at[z_near[k] * NX + x]
        return remote(near_w, near_w, wz_send.at[k], wz_recv.at[z_near[k]], partner)

    def pass_z(k):
        z_rows(k).wait_recv()
        for cp in wx[k]:
            cp.start()

    def pass_half(k):
        for cp, onward in zip(wx[k], wr[k]):
            cp.wait_recv()
            onward.start()

    rest = []
    for dy in (2, 6, 1, 7):
        for j, cp in enumerate(rows_to(dy)):
            flag = is_last(dy, x, z, j)
            later_to.append(([flag], cp.start))
            rest.append((pl.when(no(flag)), cp))

    do([z_rows(1)], [], None, near_last[1])
    do([], [wx[1][0]], right_last, near_last[1])
    do([], [wx[1][1]], left_last, near_last[1])

    @pl.when(by_last)
    def _():
        pl.semaphore_wait(ready, 1)
        for flags, act in later_to:
            pl.when(functools.reduce(lambda p, q: p & q, flags))(act)

    held = []
    for j in range(NC):
        back, on = (NY - 2, 2) if j == 0 else (2, NY - 2)
        slot = ((y + back) % NY) * NC + c
        second_legs.append(remote(
            relay.at[j], recv.at[slot], a_send.at[13 + j], a_recv.at[slot],
            {"group": (y + on) % NY, "blk": blk_of(x, z, j)},
        ))
        held.append(last | is_last(back, x, z, c))

    def pass_rows(j):
        first_legs[j].wait_recv()
        second_legs[j].start()

    for unless_last, cp in rest[:4]:
        unless_last(cp.start)
    for j in range(NC):
        pl.when(no(held[j]))(functools.partial(pass_rows, j))
    for unless_last, cp in rest[4:]:
        unless_last(cp.start)
    cross = remote(send.at[y, 1 - c], recv.at[here], a_send.at[12], a_recv.at[here], partner)
    cross.start()
    pass_z(2)
    pass_half(0)
    pass_z(3)

    @pl.when(by_last)
    def _():
        for flags, act in later_from:
            pl.when(functools.reduce(lambda p, q: p & q, flags))(act)

    pass_half(1)
    for j in range(NC):
        pl.when(held[j])(functools.partial(pass_rows, j))
    pass_half(2)
    pass_half(3)
    for k in range(NZ):
        for cp in wr[k]:
            cp.wait_recv()
    own.wait()
    for n in range(1, NY * NC):
        slot = (here + n) % (NY * NC)
        remote(
            recv.at[slot], recv.at[slot], a_send.at[15], a_recv.at[slot], partner
        ).wait_recv()

    swap_cot = remote(
        recv.at[:, :, pl.ds(half, 128)], cot_other, ex_send.at[2], ex_recv.at[2], partner
    )
    swap_cot.start()
    swaps = []
    rows_here = recv[:, :, :half].reshape(NY * NC * CAP, half)
    for q in range(hid // 128):
        part[q] = dot(rows_here, w[:, :, q * 256:(q + 1) * 256].reshape(half, 256))
        part_sent[q] = part[q].astype(BF)
        cp = remote(part_sent.at[q], other.at[q], ex_send.at[q], ex_recv.at[q], partner)
        cp.start()
        swaps.append(cp)

    def backward(q):
        swaps[q].wait_recv()
        gate = part[q, :, :128] + other[q, :, :128].astype(F32)
        up = part[q, :, 128:] + other[q, :, 128:].astype(F32)
        mine = recv[:, :, half:].reshape(NY * NC * CAP, 128).astype(F32)
        theirs = cot_other[...].reshape(NY * NC * CAP, 128).astype(F32)
        cotangent = jnp.where(c == q, mine, theirs)
        s = jax.nn.sigmoid(gate)
        d_gate = cotangent * up * s * (1.0 + gate * (1.0 - s))
        d_up = cotangent * gate * s
        p_t[q * 256:q * 256 + 128, :] = d_gate.T.astype(BF)
        p_t[q * 256 + 128:(q + 1) * 256, :] = d_up.T.astype(BF)

    upper, lower = pl.ds(0, hid), pl.ds(hid, hid)

    def z_of(k):
        return z_near[NZ - 1 - k]

    def product(k, halves=(0, 1)):
        zz = z_of(k)
        cols = recv[:, :, pl.ds(pl.multiple_of(zz * (NX * 128), 128), NX * 128)].reshape(
            NY * NC * CAP, NX * 128
        )
        for m in halves:
            got = dot(p_t[m * hid:(m + 1) * hid, :], cols).astype(BF)
            for xx in range(NX):
                g[zz, xx, m * hid:(m + 1) * hid, :] = got[:, xx * 128:(xx + 1) * 128]

    def sends(k):
        zz = z_of(k)
        return [
            remote(g.at[zz, across, upper], r_a.at[zz], rs_send.at[0, k], rs_recv.at[0, k], to_right),
            remote(g.at[zz, across, lower], r_b.at[zz], rs_send.at[1, k], rs_recv.at[1, k], to_left),
            remote(g.at[zz, right, lower], f_l.at[zz, lower], rs_send.at[2, k], rs_recv.at[2, k], to_right),
            remote(g.at[zz, left, upper], f_r.at[zz, upper], rs_send.at[3, k], rs_recv.at[3, k], to_left),
            remote(g.at[zz, right, upper], f_l.at[zz, upper], rs_send.at[4, k], rs_recv.at[4, k], to_right),
            remote(g.at[zz, left, lower], f_r.at[zz, lower], rs_send.at[5, k], rs_recv.at[5, k], to_left),
        ]

    rs = [sends(k) for k in range(NZ)]
    zs = [
        remote(
            g.at[z_of(k), x], z_buf.at[z], z_send.at[k], z_recv.at[z],
            {"blk": blk_of(x, z_of(k), c)},
        )
        for k in range(NZ - 1)
    ]

    def far_start(k):
        product(k)
        for cp in rs[k][:2]:
            cp.start()

    def near_start(k):
        for cp in rs[k][2:4]:
            cp.start()

    def pass_on(k):
        zz = z_of(k)
        rs[k][0].wait_recv()
        g[zz, right, upper] = (g[zz, right, upper].astype(F32) + r_a[zz].astype(F32)).astype(BF)
        rs[k][4].start()
        rs[k][1].wait_recv()
        g[zz, left, lower] = (g[zz, left, lower].astype(F32) + r_b[zz].astype(F32)).astype(BF)
        rs[k][5].start()

    def gathered(k):
        zz = z_of(k)
        for cp in rs[k][2:]:
            cp.wait_recv()
        return g[zz, x].astype(F32) + f_l[zz].astype(F32) + f_r[zz].astype(F32)

    def finish(k):
        g[z_of(k), x] = gathered(k).astype(BF)
        zs[k].start()

    swap_cot.wait_recv()
    backward(0)
    product(0, (0,))
    rs[0][0].start()
    rs[0][3].start()
    product(1, (0,))
    rs[1][0].start()
    backward(1)
    product(0, (1,))
    rs[0][1].start()
    rs[0][2].start()
    product(1, (1,))
    rs[1][1].start()
    pass_on(0)
    near_start(1)
    far_start(2)
    pass_on(1)
    finish(0)
    near_start(2)
    far_start(3)
    pass_on(2)
    near_start(3)
    finish(1)
    pass_on(3)
    finish(2)
    def from_z(k):
        got = z_buf.at[z_near[k]]
        remote(got, got, z_send.at[k], z_recv.at[z_near[k]], partner).wait_recv()
        return got[...].astype(F32)

    total = from_z(3) + gathered(NZ - 1)
    total = total + from_z(2) + from_z(1)
    for q in range(hid // 128):
        for j in range(2):
            out_ref[:, j * hid + q * 128:j * hid + (q + 1) * 128] = (
                total[q * 256 + j * 128:q * 256 + (j + 1) * 128].T.astype(BF)
            )

    for cp in wz[1:] + direct + first_legs + second_legs + swaps + zs + [swap_cot, cross]:
        cp.wait_send()
    for group in wx + wr + rs:
        for cp in group:
            cp.wait_send()


def local(tokens, routed_experts, act_cotangent, weight_codes, weight_scales):
    rows, width = tokens.shape
    top, hid = act_cotangent.shape[1:]
    half = width // 2
    dma = pltpu.SemaphoreType.DMA
    hbm = pl.BlockSpec(memory_space=pltpu.HBM)
    out = pl.pallas_call(
        kernel,
        out_shape=jax.ShapeDtypeStruct((rows, 2 * hid), BF),
        in_specs=[hbm] * 5,
        out_specs=pl.BlockSpec(memory_space=pltpu.VMEM),
        scratch_shapes=[
            pltpu.VMEM((rows, width), BF),
            pltpu.VMEM((top, rows), jnp.int32),
            pltpu.VMEM((rows * top, hid), BF),
            pltpu.VMEM((rows, 1, 2, hid), BF),
            pltpu.VMEM((1, 1, 2, hid // 128), BF),
            pltpu.VMEM((rows, 2, hid), F32),
            pltpu.VMEM((rows, top, 128), F32),
            pltpu.VMEM((NY, NC, CAP, half + 128), BF),
            pltpu.VMEM((NY * NC, CAP, half + 128), BF),
            pltpu.VMEM((NC, CAP, half + 128), BF),
            pltpu.VMEM((NX * NZ, 128, 2 * hid), BF),
            pltpu.VMEM((2, NY * NC * CAP, hid), F32),
            pltpu.VMEM((2, NY * NC * CAP, hid), BF),
            pltpu.VMEM((2, NY * NC * CAP, hid), BF),
            pltpu.VMEM((NY * NC, CAP, 128), BF),
            pltpu.VMEM((2 * hid, NY * NC * CAP), BF),
            pltpu.VMEM((NZ, NX, 2 * hid, 128), BF),
            pltpu.VMEM((NZ, hid, 128), BF),
            pltpu.VMEM((NZ, hid, 128), BF),
            pltpu.VMEM((NZ, 2 * hid, 128), BF),
            pltpu.VMEM((NZ, 2 * hid, 128), BF),
            pltpu.VMEM((NZ, 2 * hid, 128), BF),
            dma((5,)), dma, pltpu.SemaphoreType.REGULAR,
            dma((16,)), dma((16,)), dma((2,)), dma((2,)),
            dma((NZ,)), dma((NZ,)), dma((4, NZ)), dma((4, NZ)),
            dma((3,)), dma((3,)),
            dma((6, NZ)), dma((6, NZ)), dma((NZ,)), dma((NZ,)),
        ],
        compiler_params=pltpu.CompilerParams(
            collective_id=0, has_side_effects=True, vmem_limit_bytes=48 * 1024 * 1024
        ),
    )(*[
        pltpu.with_memory_space_constraint(a, pltpu.HBM)
        for a in (
            tokens, routed_experts.T, act_cotangent.reshape(rows * top, hid),
            weight_codes, weight_scales,
        )
    ])
    return out.reshape(rows, 1, 2, hid)


def solution(mesh):
    return jax.shard_map(
        local,
        mesh=mesh,
        in_specs=(
            P(("group", "blk"), None),
            P(("group", "blk"), None),
            P(("group", "blk"), None, "att"),
            P("blk", "group", None, "att"),
            P("blk", "group", None, "att"),
        ),
        out_specs=P("blk", "group", None, "att"),
        check_vma=False,
    )
```
